128 devices in a mesh: ha: 2 (over z_hi), wa: 64 (over y, z_lo, x, core).
Axes of the slice: x: 4, y: 4, z: 4 (z_hi: 2, z_lo: 2; z = z_hi * 2 + z_lo), core: 2. Of those that a mesh axis runs over, the one named last changes fastest.
Arguments:
- queries: float32 [2, 16, 512, 256], P(None, 'ha', 'wa'), may hold values from -240 to 240
- keys: float32 [2, 16, 512, 256], P(None, 'ha', 'wa'), may hold values from -6 to 6
- values: float32 [2, 16, 512, 256], P(None, 'ha', 'wa'), may hold values from -6 to 6
- cotangent: float32 [2, 16, 512, 256], P(None, 'ha', 'wa'), may hold values from -6 to 6
Outputs:
- query_grad: float32 [2, 16, 512, 256], P(None, 'ha', 'wa')
- key_grad: float32 [2, 16, 512, 256], P(None, 'ha', 'wa')
- value_grad: float32 [2, 16, 512, 256], P(None, 'ha', 'wa')
The draws below stay inside these ranges and needn't reach their ends.
All inputs are finite; a program needn't handle non-finite values.
Results may differ from the reference program's by a relative error of at most 0.0003.
Values sent between devices are 32-bit elements; how exact they have to be, the bound alone decides.
A program may use at most 128 MiB of HBM per device.

```python
import math
import jax
import jax.numpy as jnp
from jax import lax

HEADS = 4
HEAD_DIM = 64
CHANNELS = 256
IMAGES = 2
GRID_ROWS = 16
GRID_COLS = 512


def shared_fields(key):
    shape = (IMAGES, GRID_ROWS, GRID_COLS, CHANNELS)
    basis = jnp.clip(jax.random.normal(jax.random.fold_in(key, 11), shape, jnp.float32), -6.0, 6.0)
    return basis


def draw_keys(key, part):
    basis = shared_fields(key)
    return basis


def draw_queries(key, part):
    shape = (IMAGES, GRID_ROWS, GRID_COLS, CHANNELS)
    fresh = jnp.clip(jax.random.normal(jax.random.fold_in(key, 15), shape, jnp.float32), -6.0, 6.0)
    return fresh


def levels(stream_key, shape, cuts, least, top_value):
    gain = 1.0
    for dim, blocks in cuts:
        draws = jax.random.uniform(jax.random.fold_in(jax.random.fold_in(stream_key, 6), dim), (blocks,), jnp.float32, least / len(cuts), top_value / len(cuts))
        gain = gain * jnp.repeat(jnp.exp(draws), shape[dim] // blocks).reshape((-1,) + (1,) * (len(shape) - 1 - dim))
    return gain


def bell_draw(own_key, shape, deviation, most, pieces=(), kind=jnp.bfloat16):
    values = jax.random.normal(own_key, shape, jnp.float32) * deviation
    if len(pieces) > 0:
        values = levels(own_key, shape, pieces, -0.22, 0.18) * values
    return jnp.clip(values, min=-most, max=most).astype(kind)


def setup_inputs(seed: int = 0) -> dict:
    streams_of = jax.random.split(jax.random.key(seed), 5)
    return {
        "queries": draw_queries(jax.random.fold_in(streams_of[4], 71), 0),
        "keys": draw_keys(jax.random.fold_in(streams_of[4], 71), 0),
        "values": bell_draw(streams_of[2], (IMAGES, GRID_ROWS, GRID_COLS, CHANNELS), 1.0, 6.0, ((1, 2), (2, 64)), jnp.float32),
        "cotangent": bell_draw(streams_of[3], (IMAGES, GRID_ROWS, GRID_COLS, CHANNELS), 1.0, 6.0, ((1, 2), (2, 64)), jnp.float32),
    }


def single_image(queries, keys, values, cotangent):
    grid_rows = queries.shape[0]
    grid_cols = queries.shape[1]
    scale = 1.0 / math.sqrt(HEAD_DIM)
    split = (grid_rows, grid_cols, HEADS, HEAD_DIM)
    query_heads = queries.reshape(split)
    cot_heads = cotangent.reshape(split)
    widths = ((3, 3), (3, 3), (0, 0), (0, 0))
    key_pad = jnp.pad(keys.reshape(split), widths)
    value_pad = jnp.pad(values.reshape(split), widths)
    inside = jnp.pad(jnp.ones((grid_rows, grid_cols), dtype=bool), 3)
    offsets = [(row_off, col_off) for row_off in range(7) for col_off in range(7)]
    score_list = []
    for row_off, col_off in offsets:
        shifted = key_pad[row_off:row_off + grid_rows, col_off:col_off + grid_cols]
        score = lax.optimization_barrier(jnp.sum(query_heads * shifted, axis=-1)) * scale
        live = inside[row_off:row_off + grid_rows, col_off:col_off + grid_cols][:, :, None]
        score_list.append(jnp.where(live, score, -jnp.inf))
    scores = jnp.stack(score_list)
    top = lax.optimization_barrier(jnp.max(scores, axis=0))
    expd = jnp.exp(scores - top[None])
    probs = expd / lax.optimization_barrier(jnp.sum(expd, axis=0))[None]
    attended = jnp.zeros(split, jnp.float32)
    for index, (row_off, col_off) in enumerate(offsets):
        shifted = value_pad[row_off:row_off + grid_rows, col_off:col_off + grid_cols]
        attended = attended + probs[index][..., None] * shifted
    delta = lax.optimization_barrier(jnp.sum(cot_heads * attended, axis=-1))
    query_grad = jnp.zeros(split, jnp.float32)
    key_acc = jnp.zeros(key_pad.shape, jnp.float32)
    value_acc = jnp.zeros(value_pad.shape, jnp.float32)
    for index, (row_off, col_off) in enumerate(offsets):
        vshift = value_pad[row_off:row_off + grid_rows, col_off:col_off + grid_cols]
        kshift = key_pad[row_off:row_off + grid_rows, col_off:col_off + grid_cols]
        dprob = lax.optimization_barrier(jnp.sum(cot_heads * vshift, axis=-1))
        dscore = probs[index] * (dprob - delta)
        query_grad = query_grad + scale * dscore[..., None] * kshift
        key_acc = key_acc.at[row_off:row_off + grid_rows, col_off:col_off + grid_cols].add(scale * dscore[..., None] * query_heads)
        value_acc = value_acc.at[row_off:row_off + grid_rows, col_off:col_off + grid_cols].add(probs[index][..., None] * cot_heads)
    flat = (grid_rows, grid_cols, HEADS * HEAD_DIM)
    key_grad = key_acc[3:3 + grid_rows, 3:3 + grid_cols].reshape(flat)
    value_grad = value_acc[3:3 + grid_rows, 3:3 + grid_cols].reshape(flat)
    return (query_grad.reshape(flat), key_grad, value_grad)

def reference(queries, keys, values, cotangent):
    query_grad, key_grad, value_grad = jax.vmap(single_image)(queries, keys, values, cotangent)
    return (query_grad, key_grad, value_grad)
```

```python
import functools

import jax
import jax.numpy as jnp
from jax import lax
from jax.experimental import pallas as pl
from jax.experimental.pallas import tpu as pltpu
from jax.sharding import PartitionSpec as P

HEADS = 4
REACH = 3
MESH = pl.DeviceIdType.MESH
HIGHEST = lax.Precision.HIGHEST

OWN = 0
LEFT = 64
RIGHT = 88
ROWS = 112
CORNER_LEFT = 136
CORNER_RIGHT = 152
KEYS = 168
BLOCKS = ((LEFT, 24), (RIGHT, 24), (ROWS, 24), (CORNER_LEFT, 16), (CORNER_RIGHT, 16))


def dot(a, b, contract):
    return lax.dot_general(
        a, b, (contract, ((), ())), precision=HIGHEST, preferred_element_type=jnp.float32
    )


def kernel(
    wa_count,
    q_ref,
    k_ref,
    v_ref,
    c_ref,
    dq_ref,
    dk_ref,
    dv_ref,
    wide,
    packed,
    terms,
    back,
    bias,
    qs,
    cs,
    send_sem,
    recv_sem,
    send_sem2,
    recv_sem2,
):
    images, tile_rows, tile_cols, channels = q_ref.shape
    tokens = tile_rows * tile_cols
    head_size = channels // HEADS
    ha = lax.axis_index("ha")
    wa = lax.axis_index("wa")
    other = 1 - ha
    left = lax.rem(wa + wa_count - 1, wa_count)
    right = lax.rem(wa + 1, wa_count)
    owners = ((ha, left), (ha, right), (other, wa), (other, left), (other, right))
    takers = ((ha, right), (ha, left), (other, wa), (other, right), (other, left))

    barrier = pltpu.get_barrier_semaphore()
    for device in owners:
        pl.semaphore_signal(barrier, inc=1, device_id=device, device_id_type=MESH)

    edge = (tile_rows - REACH) * other

    def edge_row(index):
        return pl.multiple_of((edge + index) * tile_cols, tile_cols)

    for image in range(images):
        for field, ref in enumerate((k_ref, v_ref)):
            own = ref[image].reshape(tokens, channels)
            wide[image, field, OWN : OWN + tokens] = own
            for row in range(tile_rows):
                line = own[row * tile_cols : (row + 1) * tile_cols]
                packed[image, 0, field, 3 * row : 3 * row + 3] = line[tile_cols - REACH :]
                packed[image, 1, field, 3 * row : 3 * row + 3] = line[:REACH]
            for row in range(REACH):
                line = wide[image, field, pl.ds(edge_row(row), tile_cols)]
                packed[image, 2, field, 3 * row : 3 * row + 3] = line[tile_cols - REACH :]
                packed[image, 3, field, 3 * row : 3 * row + 3] = line[:REACH]
            for side in (2, 3):
                packed[image, side, field, 9:16] = jnp.zeros((7, channels), jnp.float32)

    pl.semaphore_wait(barrier, len(owners))

    halo = []
    for image in range(images):
        copies = []
        for block, (first, size) in enumerate(BLOCKS):
            if block == 2:
                source = wide.at[image, :, pl.ds(edge_row(0), size)]
            else:
                slot = block if block < 2 else block - 1
                source = packed.at[image, slot, :, pl.ds(0, size)]
            copy = pltpu.make_async_remote_copy(
                src_ref=source,
                dst_ref=wide.at[image, :, pl.ds(first, size)],
                send_sem=send_sem.at[image, block],
                recv_sem=recv_sem.at[image, block],
                device_id=takers[block],
                device_id_type=MESH,
            )
            copy.start()
            copies.append(copy)
        halo.append(copies)

    def coordinates(first, size):
        key = lax.broadcasted_iota(jnp.int32, (size, channels), 0)
        row_base = jnp.where(ha == 0, tile_rows, -REACH)
        third = (key * 11) >> 5
        if first == OWN:
            return key >> 3, key & 7, None
        if first == LEFT:
            return third, key - 3 * third - REACH, wa > 0
        if first == RIGHT:
            return third, key - 3 * third + tile_cols, wa < wa_count - 1
        if first == ROWS:
            return row_base + (key >> 3), key & 7, None
        row = jnp.where(key < 9, row_base + third, 100)
        if first == CORNER_LEFT:
            return row, key - 3 * third - REACH, wa > 0
        return row, key - 3 * third + tile_cols, wa < wa_count - 1

    for first, size in ((OWN, tokens),) + BLOCKS:
        key_row, key_col, live = coordinates(first, size)
        token = lax.broadcasted_iota(jnp.int32, (size, channels), 1) & (tokens - 1)
        row_gap = jnp.abs(key_row - (token >> 3))
        col_gap = jnp.abs(key_col - (token & 7))
        gap = jnp.maximum(row_gap, col_gap)
        if live is not None:
            gap = gap + jnp.where(live, 0, 100)
        bias[first : first + size] = jnp.where(gap <= REACH, 0.0, -1e30)

    lane_head = lax.broadcasted_iota(jnp.int32, (tokens, channels), 1) // head_size
    scale = 1.0 / 8.0
    for image in range(images):
        query = q_ref[image].reshape(tokens, channels) * scale
        cot = c_ref[image].reshape(tokens, channels)
        for head in range(HEADS):
            mine = lane_head == head
            qs[image, head * tokens : (head + 1) * tokens] = jnp.where(mine, query, 0.0)
            cs[image, head * tokens : (head + 1) * tokens] = jnp.where(mine, cot, 0.0)

    returned = []
    for image in range(images):
        for copy in halo[image]:
            copy.wait_recv()
        keys = wide[image, 0]
        values = wide[image, 1]
        scores = dot(keys, qs[image], ((1,), (1,))) + bias[...]
        dprobs = dot(values, cs[image], ((1,), (1,)))
        top = jnp.max(scores, axis=0, keepdims=True)
        expd = jnp.exp(scores - top)
        probs = expd / jnp.sum(expd, axis=0, keepdims=True)
        delta = jnp.sum(probs * dprobs, axis=0, keepdims=True)
        dscores = probs * (dprobs - delta)
        terms[image, 0] = dot(dscores, qs[image], ((1,), (0,)))
        terms[image, 1] = dot(probs, cs[image], ((1,), (0,)))
        copies = []
        for block, (first, size) in enumerate(BLOCKS):
            copy = pltpu.make_async_remote_copy(
                src_ref=terms.at[image, :, pl.ds(first, size)],
                dst_ref=back.at[image, :, pl.ds(first - tokens, size)],
                send_sem=send_sem2.at[image, block],
                recv_sem=recv_sem2.at[image, block],
                device_id=owners[block],
                device_id_type=MESH,
            )
            copy.start()
            copies.append(copy)
        returned.append(copies)
        spread = dot(dscores, keys, ((0,), (0,)))
        total = jnp.zeros((tokens, channels), jnp.float32)
        for head in range(HEADS):
            total = total + jnp.where(
                lane_head == head, spread[head * tokens : (head + 1) * tokens], 0.0
            )
        dq_ref[image] = (total * scale).reshape(tile_rows, tile_cols, channels)
        for field, ref in enumerate((dk_ref, dv_ref)):
            ref[image] = terms[image, field, OWN : OWN + tokens].reshape(
                tile_rows, tile_cols, channels
            )

    high = pl.ds(tile_cols - REACH, REACH)
    low = pl.ds(0, REACH)
    for image in range(images):
        for copy in returned[image]:
            copy.wait_recv()
        for field, ref in enumerate((dk_ref, dv_ref)):
            for row in range(tile_rows):
                ref[image, row, high] += back[image, field, pl.ds(LEFT - tokens + 3 * row, 3)]
                ref[image, row, low] += back[image, field, pl.ds(RIGHT - tokens + 3 * row, 3)]
            for row in range(REACH):
                at = edge + row
                ref[image, at] += back[image, field, pl.ds(ROWS - tokens + 8 * row, 8)]
                ref[image, at, high] += back[
                    image, field, pl.ds(CORNER_LEFT - tokens + 3 * row, 3)
                ]
                ref[image, at, low] += back[
                    image, field, pl.ds(CORNER_RIGHT - tokens + 3 * row, 3)
                ]
    for copies in halo + returned:
        for copy in copies:
            copy.wait_send()


def per_device(wa_count, queries, keys, values, cotangent):
    images, tile_rows, tile_cols, channels = queries.shape
    out = jax.ShapeDtypeStruct(queries.shape, jnp.float32)
    vmem = pl.BlockSpec(memory_space=pltpu.VMEM)
    sems = pltpu.SemaphoreType.DMA((images, len(BLOCKS)))
    return pl.pallas_call(
        functools.partial(kernel, wa_count),
        out_shape=(out, out, out),
        in_specs=[vmem] * 4,
        out_specs=(vmem,) * 3,
        scratch_shapes=[
            pltpu.VMEM((images, 2, KEYS, channels), jnp.float32),
            pltpu.VMEM((images, 4, 2, 24, channels), jnp.float32),
            pltpu.VMEM((images, 2, KEYS, channels), jnp.float32),
            pltpu.VMEM((images, 2, KEYS - 64, channels), jnp.float32),
            pltpu.VMEM((KEYS, channels), jnp.float32),
            pltpu.VMEM((images, 256, channels), jnp.float32),
            pltpu.VMEM((images, 256, channels), jnp.float32),
            sems,
            sems,
            sems,
            sems,
        ],
        compiler_params=pltpu.CompilerParams(collective_id=0, has_side_effects=True),
    )(queries, keys, values, cotangent)


def solution(mesh):
    spec = P(None, "ha", "wa", None)
    return jax.shard_map(
        functools.partial(per_device, mesh.shape["wa"]),
        mesh=mesh,
        in_specs=(spec,) * 4,
        out_specs=(spec,) * 3,
        check_vma=False,
    )
```

```python
import functools

import jax
import jax.numpy as jnp
from jax import lax
from jax.experimental import pallas as pl
from jax.experimental.pallas import tpu as pltpu
from jax.sharding import PartitionSpec as P

HEADS = 4
REACH = 3
MESH = pl.DeviceIdType.MESH
HIGHEST = lax.Precision.HIGHEST

TILE = 8
TOKENS = 64
LEFT = 64
RIGHT = 88
ROWS = 112
CORNER_LEFT = 136
CORNER_RIGHT = 152
WIDE = 168
SLOTS = 32
OUTER = 512
KEY, VALUE, QUERY, COT = range(4)
SCALE = 1.0 / 8.0


def dot(a, b, contract):
    return lax.dot_general(
        a, b, (contract, ((), ())), precision=HIGHEST, preferred_element_type=jnp.float32
    )


def third(index):
    return (index * 11) >> 5


def kernel(
    wa_count,
    q_hbm,
    k_hbm,
    v_hbm,
    c_hbm,
    dq_ref,
    dk_ref,
    dv_ref,
    wide,
    packed,
    corners,
    bias,
    outer_bias,
    pick,
    qs,
    cs,
    outer_q,
    outer_c,
    stats_out,
    stats_in,
    load_sem,
    row_sem,
    col_sem,
    corner_sem,
    stat_sem,
):
    images, tokens, channels = q_hbm.shape
    head_size = channels // HEADS
    ha = lax.axis_index("ha")
    wa = lax.axis_index("wa")
    other = 1 - ha
    has_left = wa > 0
    has_right = wa < wa_count - 1
    left = jnp.maximum(wa - 1, 0)
    right = jnp.minimum(wa + 1, wa_count - 1)

    barrier = pltpu.get_barrier_semaphore()

    def greet(device):
        pl.semaphore_signal(barrier, inc=1, device_id=device, device_id_type=MESH)

    greet((other, wa))

    @pl.when(has_left)
    def _():
        greet((other, left))
        greet((ha, left))

    @pl.when(has_right)
    def _():
        greet((other, right))
        greet((ha, right))

    loads = []
    for field, ref in ((KEY, k_hbm), (VALUE, v_hbm), (QUERY, q_hbm), (COT, c_hbm)):
        load = pltpu.make_async_copy(ref, wide.at[:, field, pl.ds(0, tokens)], load_sem.at[field])
        load.start()
        loads.append(load)

    edge = (TILE - REACH) * other
    row_base = jnp.where(ha == 0, TILE, -REACH)

    def place(first, index):
        part = third(index)
        if first == 0:
            return index >> 3, index & 7, None
        if first == LEFT:
            return part, index - 3 * part - REACH, has_left
        if first == RIGHT:
            return part, index - 3 * part + TILE, has_right
        if first == ROWS:
            return row_base + (index >> 3), index & 7, None
        row = jnp.where(index < 9, row_base + part, 100)
        if first == CORNER_LEFT:
            return row, index - 3 * part - REACH, has_left
        return row, index - 3 * part + TILE, has_right

    def window(key_row, key_col, query_row, query_col, live):
        gap = jnp.maximum(jnp.abs(key_row - query_row), jnp.abs(key_col - query_col))
        if live is not None:
            gap = gap + jnp.where(live, 0, 100)
        return jnp.where(gap <= REACH, 0.0, -1e30)

    def iota(shape, dim):
        return lax.broadcasted_iota(jnp.int32, shape, dim)

    token = iota((1, channels), 1) & (tokens - 1)
    blocks = (
        (0, tokens),
        (LEFT, 24),
        (RIGHT, 24),
        (ROWS, 24),
        (CORNER_LEFT, 16),
        (CORNER_RIGHT, 16),
    )
    for first, size in blocks:
        row, col, live = place(first, iota((size, 1), 0))
        bias[first : first + size] = window(row, col, token >> 3, token & 7, live)
    own = iota((tokens, 1), 0)
    slot = iota((1, 128), 1) & (SLOTS - 1)
    for piece, first in enumerate((LEFT, RIGHT, ROWS)):
        row, col, live = place(first, jnp.minimum(slot, 23))
        row = jnp.where(slot < 24, row, 100)
        outer_bias[:, 128 * piece : 128 * piece + 128] = window(own >> 3, own & 7, row, col, live)
    low_slot = slot < 16
    row_l, col_l, _ = place(CORNER_LEFT, slot & 15)
    row_r, col_r, _ = place(CORNER_RIGHT, slot & 15)
    alive = jnp.where(low_slot, has_left.astype(jnp.int32), has_right.astype(jnp.int32)) > 0
    outer_bias[:, 384:] = window(
        own >> 3, own & 7, jnp.where(low_slot, row_l, row_r), jnp.where(low_slot, col_l, col_r), alive
    )

    part = third(jnp.minimum(slot, 23))
    within = jnp.minimum(slot, 23) - 3 * part
    part_c = third(slot & 15)
    within_c = (slot & 15) - 3 * part_c
    sources = (
        jnp.where(slot < 24, part * TILE + (TILE - REACH) + within, -1000),
        jnp.where(slot < 24, part * TILE + within, -1000),
        jnp.where(slot < 24, edge * TILE + slot, -1000),
        jnp.where(
            (slot & 15) < 9,
            (edge + part_c) * TILE + within_c + jnp.where(low_slot, TILE - REACH, 0),
            -1000,
        ),
    )
    lane_slot_head = iota((1, 128), 1) >> 5
    for piece, source in enumerate(sources):
        lane = source + lane_slot_head * tokens
        pick[:, 128 * piece : 128 * piece + 128] = jnp.where(
            iota((channels, 128), 0) == lane, 1.0, 0.0
        ).astype(jnp.bfloat16)

    def clear(first, size, piece, corner, which):
        for image in range(images):
            for field in range(4):
                wide[image, field, first : first + size] = jnp.zeros((size, channels), jnp.float32)
                wide[image, field, corner : corner + 16] = jnp.zeros((16, channels), jnp.float32)
            stats_in[image, piece] = jnp.zeros((8, 128), jnp.float32)
            stats_in[image, which] = jnp.zeros((8, 128), jnp.float32)

    pl.when(jnp.logical_not(has_left))(lambda: clear(LEFT, 24, 0, CORNER_LEFT, 3))
    pl.when(jnp.logical_not(has_right))(lambda: clear(RIGHT, 24, 1, CORNER_RIGHT, 4))

    for field in range(4):
        loads[field].wait()
        for image in range(images):
            mine = wide[image, field, 0:tokens]
            for row in range(TILE):
                line = mine[row * TILE : (row + 1) * TILE]
                packed[image, 0, field, 3 * row : 3 * row + 3] = line[TILE - REACH :]
                packed[image, 1, field, 3 * row : 3 * row + 3] = line[:REACH]

    pl.semaphore_wait(
        barrier, 1 + 2 * has_left.astype(jnp.int32) + 2 * has_right.astype(jnp.int32)
    )

    def remote(source, target, sems, index, device):
        return pltpu.make_async_remote_copy(
            src_ref=source,
            dst_ref=target,
            send_sem=sems.at[(0,) + index],
            recv_sem=sems.at[(1,) + index],
            device_id=device,
            device_id_type=MESH,
        )

    edge_start = pl.multiple_of(edge * TILE, TILE)
    pairs = ((KEY, 2), (QUERY, 2))

    def rows_copy(image, pair):
        fields = pl.ds(*pairs[pair])
        return remote(
            wide.at[image, fields, pl.ds(edge_start, 24)],
            wide.at[image, fields, pl.ds(ROWS, 24)],
            row_sem,
            (image, pair),
            (other, wa),
        )

    targets = ((ha, right), (ha, left))
    senders = (has_left, has_right)
    sends = (has_right, has_left)

    def cols_copy(image, pair, side):
        fields = pl.ds(*pairs[pair])
        return remote(
            packed.at[image, side, fields],
            wide.at[image, fields, pl.ds((LEFT, RIGHT)[side], 24)],
            col_sem,
            (image, pair, side),
            targets[side],
        )

    def corner_copy(image, pair, side):
        fields = pl.ds(*pairs[pair])
        return remote(
            corners.at[image, side, fields],
            wide.at[image, fields, pl.ds((CORNER_LEFT, CORNER_RIGHT)[side], 16)],
            corner_sem,
            (image, pair, side),
            targets[side],
        )

    stat_targets = (
        (ha, right),
        (ha, left),
        (other, wa),
        (other, right),
        (other, left),
    )
    stat_sends = (has_right, has_left, None, has_right, has_left)
    stat_arrives = (has_left, has_right, None, has_left, has_right)

    def stat_copy(image, piece):
        return remote(
            stats_out.at[image, min(piece, 3)],
            stats_in.at[image, piece],
            stat_sem,
            (image, piece),
            stat_targets[piece],
        )

    def if_(condition, action):
        if condition is None:
            action()
        else:
            pl.when(condition)(action)

    for pair in range(2):
        for image in range(images):
            rows_copy(image, pair).start()
        for image in range(images):
            for side in range(2):
                if_(sends[side], cols_copy(image, pair, side).start)

    lane_head = iota((tokens, channels), 1) // head_size
    for image in range(images):
        query = wide[image, QUERY, 0:tokens] * SCALE
        cot = wide[image, COT, 0:tokens]
        for head in range(HEADS):
            mine = lane_head == head
            qs[image, head * tokens : (head + 1) * tokens] = jnp.where(mine, query, 0.0)
            cs[image, head * tokens : (head + 1) * tokens] = jnp.where(mine, cot, 0.0)

    def forward(image, pair):
        rows_copy(image, pair).wait_recv()
        for field in range(2 * pair, 2 * pair + 2):
            for row in range(REACH):
                line = wide[image, field, ROWS + TILE * row : ROWS + TILE * (row + 1)]
                corners[image, 0, field, 3 * row : 3 * row + 3] = line[TILE - REACH :]
                corners[image, 1, field, 3 * row : 3 * row + 3] = line[:REACH]
            for side in range(2):
                corners[image, side, field, 9:16] = jnp.zeros((7, channels), jnp.float32)
        for side in range(2):
            if_(sends[side], corner_copy(image, pair, side).start)

    def arrived(image, pair):
        for side in range(2):
            if_(senders[side], cols_copy(image, pair, side).wait_recv)
        for side in range(2):
            if_(senders[side], corner_copy(image, pair, side).wait_recv)

    def inner(image):
        keys = wide[image, KEY]
        scores = dot(keys, qs[image], ((1,), (1,))) + bias[...]
        dprobs = dot(wide[image, VALUE], cs[image], ((1,), (1,)))
        top = jnp.max(scores, axis=0, keepdims=True)
        expd = jnp.exp(scores - top)
        norm = 1.0 / jnp.sum(expd, axis=0, keepdims=True)
        probs = expd * norm
        delta = jnp.sum(probs * dprobs, axis=0, keepdims=True)
        dscores = probs * (dprobs - delta)

        sheet = jnp.concatenate([top, norm, delta, jnp.zeros((5, channels), jnp.float32)], axis=0)
        high = sheet.astype(jnp.bfloat16)
        rest = sheet - high.astype(jnp.float32)
        middle = rest.astype(jnp.bfloat16)
        low = (rest - middle.astype(jnp.float32)).astype(jnp.bfloat16)
        picked = [
            lax.dot_general(
                term, pick[...], (((1,), (0,)), ((), ())), preferred_element_type=jnp.float32
            )
            for term in (high, middle, low)
        ]
        moved = picked[0] + picked[1] + picked[2]
        for piece in range(4):
            stats_out[image, piece] = moved[:, 128 * piece : 128 * piece + 128]
        for piece in range(5):
            if_(stat_sends[piece], stat_copy(image, piece).start)

        spread = dot(dscores, keys, ((0,), (0,)))
        total = jnp.zeros((tokens, channels), jnp.float32)
        for head in range(HEADS):
            total = total + jnp.where(
                lane_head == head, spread[head * tokens : (head + 1) * tokens], 0.0
            )
        dq_ref[image] = total * SCALE
        dk_ref[image] = dot(dscores[:tokens], qs[image], ((1,), (0,)))
        dv_ref[image] = dot(probs[:tokens], cs[image], ((1,), (0,)))

    def outer(image):
        for field, stack, factor in ((QUERY, outer_q, SCALE), (COT, outer_c, 1.0)):
            for piece, first in enumerate((LEFT, RIGHT, ROWS)):
                block = wide[image, field, first : first + 24] * factor
                for head in range(HEADS):
                    base = 128 * piece + SLOTS * head
                    stack[base : base + 24] = jnp.where(lane_head[:24] == head, block, 0.0)
                    stack[base + 24 : base + 32] = jnp.zeros((8, channels), jnp.float32)
            for half, first in enumerate((CORNER_LEFT, CORNER_RIGHT)):
                block = wide[image, field, first : first + 16] * factor
                for head in range(HEADS):
                    base = 384 + SLOTS * head + 16 * half
                    stack[base : base + 16] = jnp.where(lane_head[:16] == head, block, 0.0)
        scores = dot(wide[image, KEY, 0:tokens], outer_q[...], ((1,), (1,))) + outer_bias[...]
        dprobs = dot(wide[image, VALUE, 0:tokens], outer_c[...], ((1,), (1,)))
        for piece in range(5):
            if_(stat_arrives[piece], stat_copy(image, piece).wait_recv)
        sheet = jnp.concatenate(
            [stats_in[image, 0], stats_in[image, 1], stats_in[image, 2]]
            + [jnp.where(low_slot, stats_in[image, 3], stats_in[image, 4])],
            axis=1,
        )
        probs = jnp.exp(scores - sheet[0:1]) * sheet[1:2]
        dscores = probs * (dprobs - sheet[2:3])
        dk_ref[image] += dot(dscores, outer_q[...], ((1,), (0,)))
        dv_ref[image] += dot(probs, outer_c[...], ((1,), (0,)))

    for image in range(images):
        forward(image, 0)
    arrived(0, 0)
    inner(0)
    for image in range(images):
        forward(image, 1)
    arrived(1, 0)
    inner(1)
    for image in range(images):
        arrived(image, 1)
        outer(image)

    for image in range(images):
        for pair in range(2):
            rows_copy(image, pair).wait_send()
            for side in range(2):
                if_(sends[side], cols_copy(image, pair, side).wait_send)
                if_(sends[side], corner_copy(image, pair, side).wait_send)
        for piece in range(5):
            if_(stat_sends[piece], stat_copy(image, piece).wait_send)


def per_device(wa_count, queries, keys, values, cotangent):
    images, tile_rows, tile_cols, channels = queries.shape
    flat = (images, tile_rows * tile_cols, channels)
    f32 = jnp.float32
    out = jax.ShapeDtypeStruct(flat, f32)
    sems = pltpu.SemaphoreType.DMA
    results = pl.pallas_call(
        functools.partial(kernel, wa_count),
        out_shape=(out, out, out),
        in_specs=[pl.BlockSpec(memory_space=pl.ANY)] * 4,
        out_specs=(pl.BlockSpec(memory_space=pltpu.VMEM),) * 3,
        scratch_shapes=[
            pltpu.VMEM((images, 4, WIDE, channels), f32),
            pltpu.VMEM((images, 2, 4, 24, channels), f32),
            pltpu.VMEM((images, 2, 4, 16, channels), f32),
            pltpu.VMEM((WIDE, channels), f32),
            pltpu.VMEM((TOKENS, OUTER), f32),
            pltpu.VMEM((channels, OUTER), jnp.bfloat16),
            pltpu.VMEM((images, HEADS * TOKENS, channels), f32),
            pltpu.VMEM((images, HEADS * TOKENS, channels), f32),
            pltpu.VMEM((OUTER, channels), f32),
            pltpu.VMEM((OUTER, channels), f32),
            pltpu.VMEM((images, 4, 8, 128), f32),
            pltpu.VMEM((images, 5, 8, 128), f32),
            sems((4,)),
            sems((2, images, 2)),
            sems((2, images, 2, 2)),
            sems((2, images, 2, 2)),
            sems((2, images, 5)),
        ],
        compiler_params=pltpu.CompilerParams(collective_id=0, has_side_effects=True),
    )(*(x.reshape(flat) for x in (queries, keys, values, cotangent)))
    return tuple(x.reshape(queries.shape) for x in results)


def solution(mesh):
    spec = P(None, "ha", "wa", None)
    return jax.shard_map(
        functools.partial(per_device, mesh.shape["wa"]),
        mesh=mesh,
        in_specs=(spec,) * 4,
        out_specs=(spec,) * 3,
        check_vma=False,
    )
```

```python
import functools

import jax
import jax.numpy as jnp
from jax import lax
from jax.experimental import pallas as pl
from jax.experimental.pallas import tpu as pltpu
from jax.sharding import PartitionSpec as P

HEADS = 4
REACH = 3
MESH = pl.DeviceIdType.MESH

TILE = 8
TOKENS = 64
LEFT = 64
RIGHT = 88
ROWS = 112
CORNER_LEFT = 136
CORNER_RIGHT = 152
FULL = 168
WIDE = 176
OUTER = WIDE - TOKENS
KEY, VALUE, QUERY, COT = range(4)
SCALE = 1.0 / 8.0


def dot(a, b, contract):
    return lax.dot_general(a, b, (contract, ((), ())), preferred_element_type=jnp.float32)


def split(x, parts):
    out = []
    for index in range(parts):
        part = x.astype(jnp.bfloat16)
        out.append(part)
        if index + 1 < parts:
            x = x - part.astype(jnp.float32)
    return out


def beside(parts, order):
    return jnp.concatenate([parts[index] for index in order], axis=1)


def below(parts, order):
    return jnp.concatenate([parts[index] for index in order], axis=0)


def product(a, b, order, contract):
    left = beside if contract[0][0] else below
    right = beside if contract[1][0] else below
    return dot(left(a, [i for i, _ in order]), right(b, [j for _, j in order]), contract)


SIX = ((2, 0), (0, 2), (1, 1), (1, 0), (0, 1), (0, 0))
THREE = ((1, 0), (0, 1), (0, 0))


def third(index):
    return (index * 11) >> 5


def kernel(
    wa_count,
    q_hbm,
    k_hbm,
    v_hbm,
    c_hbm,
    dq_ref,
    dk_ref,
    dv_ref,
    wide,
    packed,
    corners,
    bias,
    outer_bias,
    chosen,
    same_head,
    qs,
    cs,
    ks,
    vs,
    stats_out,
    stats_in,
    load_sem,
    row_sem,
    col_sem,
    corner_sem,
    stat_sem,
):
    images, tokens, channels = q_hbm.shape
    head_size = channels // HEADS
    ha = lax.axis_index("ha")
    wa = lax.axis_index("wa")
    other = 1 - ha
    has_left = wa > 0
    has_right = wa < wa_count - 1
    left = jnp.maximum(wa - 1, 0)
    right = jnp.minimum(wa + 1, wa_count - 1)

    barrier = pltpu.get_barrier_semaphore()

    def greet(device):
        pl.semaphore_signal(barrier, inc=1, device_id=device, device_id_type=MESH)

    greet((other, wa))

    @pl.when(has_left)
    def _():
        greet((other, left))
        greet((ha, left))

    @pl.when(has_right)
    def _():
        greet((other, right))
        greet((ha, right))

    loads = []
    for field, ref in ((KEY, k_hbm), (VALUE, v_hbm), (QUERY, q_hbm), (COT, c_hbm)):
        load = pltpu.make_async_copy(ref, wide.at[:, field, pl.ds(0, tokens)], load_sem.at[field])
        load.start()
        loads.append(load)

    edge = (TILE - REACH) * other
    row_base = jnp.where(ha == 0, TILE, -REACH)

    def place(first, index):
        part = third(index)
        if first == 0:
            return index >> 3, index & 7, None
        if first == LEFT:
            return part, index - 3 * part - REACH, has_left
        if first == RIGHT:
            return part, index - 3 * part + TILE, has_right
        if first == ROWS:
            return row_base + (index >> 3), index & 7, None
        row = jnp.where(index < 9, row_base + part, 100)
        if first == CORNER_LEFT:
            return row, index - 3 * part - REACH, has_left
        return row, index - 3 * part + TILE, has_right

    def window(key_row, key_col, query_row, query_col, live):
        gap = jnp.maximum(jnp.abs(key_row - query_row), jnp.abs(key_col - query_col))
        if live is not None:
            gap = gap + jnp.where(live, 0, 100)
        return jnp.where(gap <= REACH, 0.0, -1e30)

    def iota(shape, dim):
        return lax.broadcasted_iota(jnp.int32, shape, dim)

    token = iota((1, channels), 1) & (tokens - 1)
    blocks = (
        (0, tokens),
        (LEFT, 24),
        (RIGHT, 24),
        (ROWS, 24),
        (CORNER_LEFT, 16),
        (CORNER_RIGHT, 16),
    )
    lane_token = iota((1, channels), 1) & (tokens - 1)
    for first, size in blocks:
        row, col, live = place(first, iota((size, 1), 0))
        bias[first : first + size] = window(row, col, token >> 3, token & 7, live)
        if first:
            low = first - tokens
            outer_bias[low : low + size] = window(
                lane_token >> 3, lane_token & 7, row, col, live
            )
            col = (col + TILE) & 7
            row = jnp.where(row < 0, row + TILE, row) & 7 if first >= ROWS else row
            chosen[low : low + size] = jnp.where(lane_token == row * TILE + col, 1.0, 0.0)
    bias[FULL:WIDE] = jnp.full((WIDE - FULL, channels), -1e30, jnp.float32)
    outer_bias[FULL - tokens :] = jnp.full((WIDE - FULL, channels), -1e30, jnp.float32)
    chosen[FULL - tokens :] = jnp.zeros((WIDE - FULL, channels), jnp.float32)
    same_head[...] = jnp.where(
        (iota((channels, channels), 0) >> 6) == (iota((channels, channels), 1) >> 6), 1.0, 0.0
    ).astype(jnp.bfloat16)
    for image in range(images):
        for field in range(4):
            wide[image, field, FULL:WIDE] = jnp.zeros((WIDE - FULL, channels), jnp.float32)

    def clear(first, size, piece, corner, which):
        for image in range(images):
            for field in range(4):
                wide[image, field, first : first + size] = jnp.zeros((size, channels), jnp.float32)
                wide[image, field, corner : corner + 16] = jnp.zeros((16, channels), jnp.float32)
            stats_in[image, piece] = jnp.zeros((8, channels), jnp.float32)
            stats_in[image, which] = jnp.zeros((8, channels), jnp.float32)

    pl.when(jnp.logical_not(has_left))(lambda: clear(LEFT, 24, 0, CORNER_LEFT, 3))
    pl.when(jnp.logical_not(has_right))(lambda: clear(RIGHT, 24, 1, CORNER_RIGHT, 4))

    def pack(pair):
        for field in range(2 * pair, 2 * pair + 2):
            loads[field].wait()
            for image in range(images):
                mine = wide[image, field, 0:tokens]
                for row in range(TILE):
                    line = mine[row * TILE : (row + 1) * TILE]
                    packed[image, 0, field, 3 * row : 3 * row + 3] = line[TILE - REACH :]
                    packed[image, 1, field, 3 * row : 3 * row + 3] = line[:REACH]

    pack(0)
    pl.semaphore_wait(
        barrier, 1 + 2 * has_left.astype(jnp.int32) + 2 * has_right.astype(jnp.int32)
    )

    def remote(source, target, sems, index, device):
        return pltpu.make_async_remote_copy(
            src_ref=source,
            dst_ref=target,
            send_sem=sems.at[(0,) + index],
            recv_sem=sems.at[(1,) + index],
            device_id=device,
            device_id_type=MESH,
        )

    edge_start = pl.multiple_of(edge * TILE, TILE)
    pairs = ((KEY, 2), (QUERY, 2))

    def rows_copy(image, pair):
        fields = pl.ds(*pairs[pair])
        return remote(
            wide.at[image, fields, pl.ds(edge_start, 24)],
            wide.at[image, fields, pl.ds(ROWS, 24)],
            row_sem,
            (image, pair),
            (other, wa),
        )

    targets = ((ha, right), (ha, left))
    senders = (has_left, has_right)
    sends = (has_right, has_left)

    def cols_copy(image, pair, side):
        fields = pl.ds(*pairs[pair])
        return remote(
            packed.at[image, side, fields],
            wide.at[image, fields, pl.ds((LEFT, RIGHT)[side], 24)],
            col_sem,
            (image, pair, side),
            targets[side],
        )

    def corner_copy(image, pair, side):
        fields = pl.ds(*pairs[pair])
        return remote(
            corners.at[image, side, fields],
            wide.at[image, fields, pl.ds((CORNER_LEFT, CORNER_RIGHT)[side], 16)],
            corner_sem,
            (image, pair, side),
            targets[side],
        )

    stat_targets = (
        (ha, right),
        (ha, left),
        (other, wa),
        (other, right),
        (other, left),
    )
    stat_sends = (has_right, has_left, None, has_right, has_left)
    stat_arrives = (has_left, has_right, None, has_left, has_right)

    def stat_copy(image, piece):
        return remote(
            stats_out.at[image],
            stats_in.at[image, piece],
            stat_sem,
            (image, piece),
            stat_targets[piece],
        )

    def if_(condition, action):
        if condition is None:
            action()
        else:
            pl.when(condition)(action)

    for pair in range(2):
        if pair:
            pack(pair)
        for image in range(images):
            rows_copy(image, pair).start()
        for image in range(images):
            for side in range(2):
                if_(sends[side], cols_copy(image, pair, side).start)

    lane_head = iota((tokens, channels), 1) // head_size
    heads = [jnp.where(lane_head == head, 1.0, 0.0).astype(jnp.bfloat16) for head in range(HEADS)]
    for image in range(images):
        for field, stack, factor, parts in (
            (QUERY, qs, SCALE, 3),
            (COT, cs, 1.0, 2),
            (KEY, ks, 1.0, 3),
            (VALUE, vs, 1.0, 2),
        ):
            for index, part in enumerate(split(wide[image, field, 0:tokens] * factor, parts)):
                for head in range(HEADS):
                    stack[image, index, head * tokens : (head + 1) * tokens] = part * heads[head]

    def forward(image, pair):
        rows_copy(image, pair).wait_recv()
        for field in range(2 * pair, 2 * pair + 2):
            for row in range(REACH):
                line = wide[image, field, ROWS + TILE * row : ROWS + TILE * (row + 1)]
                corners[image, 0, field, 3 * row : 3 * row + 3] = line[TILE - REACH :]
                corners[image, 1, field, 3 * row : 3 * row + 3] = line[:REACH]
            for side in range(2):
                corners[image, side, field, 9:16] = jnp.zeros((7, channels), jnp.float32)
        for side in range(2):
            if_(sends[side], corner_copy(image, pair, side).start)

    def arrived(image, pair):
        for side in range(2):
            if_(senders[side], cols_copy(image, pair, side).wait_recv)
        for side in range(2):
            if_(senders[side], corner_copy(image, pair, side).wait_recv)

    def parts_of(ref, image, count):
        return [ref[image, index] for index in range(count)]

    def fold(stacked):
        total = jnp.zeros((tokens, channels), jnp.float32)
        for head in range(HEADS):
            total = total + jnp.where(
                lane_head == head, stacked[head * tokens : (head + 1) * tokens], 0.0
            )
        return total

    def statistics(image):
        keys = split(wide[image, KEY], 3)
        scores = product(keys, parts_of(qs, image, 3), SIX, ((1,), (1,))) + bias[...]
        values = split(wide[image, VALUE], 2)
        dprobs = product(values, parts_of(cs, image, 2), THREE, ((1,), (1,)))
        top = jnp.max(scores, axis=0, keepdims=True)
        expd = jnp.exp(scores - top)
        norm = 1.0 / jnp.sum(expd, axis=0, keepdims=True)
        probs = expd * norm
        delta = jnp.sum(probs * dprobs, axis=0, keepdims=True)
        stats_out[image, 0:1] = top
        stats_out[image, 1:2] = norm
        stats_out[image, 2:3] = delta
        stats_out[image, 3:8] = jnp.zeros((5, channels), jnp.float32)
        for piece in range(5):
            if_(stat_sends[piece], stat_copy(image, piece).start)
        return keys, probs, probs * (dprobs - delta)

    def inner(image, keys, probs, dscores):
        dparts = split(dscores, 2)
        dq_ref[image] = fold(product(dparts, keys, THREE, ((0,), (0,)))) * SCALE
        own = [part[:tokens] for part in dparts]
        dk_ref[image] = product(own, parts_of(qs, image, 2), THREE, ((1,), (0,)))
        own = split(probs[:tokens], 2)
        dv_ref[image] = product(own, parts_of(cs, image, 2), THREE, ((1,), (0,)))

    def outer(image):
        queries = split(wide[image, QUERY, tokens:WIDE] * SCALE, 3)
        cots = split(wide[image, COT, tokens:WIDE], 2)
        scores = product(queries, parts_of(ks, image, 3), SIX, ((1,), (1,))) + outer_bias[...]
        dprobs = product(cots, parts_of(vs, image, 2), THREE, ((1,), (1,)))
        return queries, cots, scores, dprobs

    def finish(image, queries, cots, scores, dprobs):
        for piece in range(5):
            if_(stat_arrives[piece], stat_copy(image, piece).wait_recv)
        spread = []
        for which in range(3):
            lines = [
                chosen[first - tokens : first - tokens + size] * stats_in[image, piece, which : which + 1]
                for piece, (first, size) in enumerate(blocks[1:])
            ]
            spread.append(jnp.concatenate(lines + [jnp.zeros((WIDE - FULL, channels), jnp.float32)], 0))
        terms = split(jnp.concatenate(spread, 0), 3)
        table = same_head[...]
        sheet = dot(beside(terms, (2, 1, 0)), below([table], (0, 0, 0)), ((1,), (0,)))
        top, norm, delta = (sheet[OUTER * index : OUTER * (index + 1)] for index in range(3))
        probs = jnp.exp(scores - top) * norm
        dscores = probs * (dprobs - delta)
        dk_ref[image] += fold(product(split(dscores, 2), queries, THREE, ((0,), (0,))))
        dv_ref[image] += fold(product(split(probs, 2), cots, THREE, ((0,), (0,))))

    for image in range(images):
        forward(image, 0)
    kept = []
    for image in range(images):
        arrived(image, 0)
        kept.append(statistics(image))
    for image in range(images):
        forward(image, 1)
    for image in range(images):
        inner(image, *kept[image])
    kept = []
    for image in range(images):
        arrived(image, 1)
        kept.append(outer(image))
    for image in range(images):
        finish(image, *kept[image])

    for image in range(images):
        for pair in range(2):
            rows_copy(image, pair).wait_send()
            for side in range(2):
                if_(sends[side], cols_copy(image, pair, side).wait_send)
                if_(sends[side], corner_copy(image, pair, side).wait_send)
        for piece in range(5):
            if_(stat_sends[piece], stat_copy(image, piece).wait_send)


def store(*refs):
    sem = refs[6]
    copies = [pltpu.make_async_copy(refs[i], refs[3 + i], sem.at[i]) for i in range(3)]
    for copy in copies:
        copy.start()
    for copy in copies:
        copy.wait()


def per_device(wa_count, queries, keys, values, cotangent):
    images, tile_rows, tile_cols, channels = queries.shape
    flat = (images, tile_rows * tile_cols, channels)
    f32 = jnp.float32
    out = jax.ShapeDtypeStruct(flat, f32)
    sems = pltpu.SemaphoreType.DMA
    results = pl.pallas_call(
        functools.partial(kernel, wa_count),
        out_shape=(pltpu.VMEM(flat, f32),) * 3,
        in_specs=[pl.BlockSpec(memory_space=pl.ANY)] * 4,
        out_specs=(pl.BlockSpec(memory_space=pltpu.VMEM),) * 3,
        scratch_shapes=[
            pltpu.VMEM((images, 4, WIDE, channels), f32),
            pltpu.VMEM((images, 2, 4, 24, channels), f32),
            pltpu.VMEM((images, 2, 4, 16, channels), f32),
            pltpu.VMEM((WIDE, channels), f32),
            pltpu.VMEM((OUTER, channels), f32),
            pltpu.VMEM((OUTER, channels), f32),
            pltpu.VMEM((channels, channels), jnp.bfloat16),
            pltpu.VMEM((images, 3, HEADS * TOKENS, channels), jnp.bfloat16),
            pltpu.VMEM((images, 2, HEADS * TOKENS, channels), jnp.bfloat16),
            pltpu.VMEM((images, 3, HEADS * TOKENS, channels), jnp.bfloat16),
            pltpu.VMEM((images, 2, HEADS * TOKENS, channels), jnp.bfloat16),
            pltpu.VMEM((images, 8, channels), f32),
            pltpu.VMEM((images, 5, 8, channels), f32),
            sems((4,)),
            sems((2, images, 2)),
            sems((2, images, 2, 2)),
            sems((2, images, 2, 2)),
            sems((2, images, 5)),
        ],
        compiler_params=pltpu.CompilerParams(collective_id=0, has_side_effects=True),
    )(*(x.reshape(flat) for x in (queries, keys, values, cotangent)))
    results = pl.pallas_call(
        store,
        out_shape=(out, out, out),
        in_specs=[pl.BlockSpec(memory_space=pltpu.VMEM)] * 3,
        out_specs=(pl.BlockSpec(memory_space=pl.ANY),) * 3,
        scratch_shapes=[sems((3,))],
    )(*(pltpu.with_memory_space_constraint(x, pltpu.VMEM) for x in results))
    return tuple(x.reshape(queries.shape) for x in results)


def solution(mesh):
    spec = P(None, "ha", "wa", None)
    return jax.shard_map(
        functools.partial(per_device, mesh.shape["wa"]),
        mesh=mesh,
        in_specs=(spec,) * 4,
        out_specs=(spec,) * 3,
        check_vma=False,
    )
```

```python
import functools

import jax
import jax.numpy as jnp
from jax import lax
from jax.experimental import pallas as pl
from jax.experimental.pallas import tpu as pltpu
from jax.sharding import PartitionSpec as P

HEADS = 4
REACH = 3
MESH = pl.DeviceIdType.MESH

TILE = 8
TOKENS = 64
EDGE = REACH * TILE
LEFT = 64
RIGHT = 88
WIDE = 112
OWN = 256
SLOTS = 32
LANES = 384
SCALE = 1.0 / 8.0
FAR = -1e30


def dot(a, b, contract):
    return lax.dot_general(a, b, (contract, ((), ())), preferred_element_type=jnp.float32)


def split(x, parts):
    out = []
    for index in range(parts):
        part = x.astype(jnp.bfloat16)
        out.append(part)
        if index + 1 < parts:
            x = x - part.astype(jnp.float32)
    return out


def beside(parts, order):
    return jnp.concatenate([parts[index] for index in order], axis=1)


def below(parts, order):
    return jnp.concatenate([parts[index] for index in order], axis=0)


def product(a, b, order, contract):
    left = beside if contract[0][0] else below
    right = beside if contract[1][0] else below
    return dot(left(a, [i for i, _ in order]), right(b, [j for _, j in order]), contract)


SIX = ((2, 0), (0, 2), (1, 1), (1, 0), (0, 1), (0, 0))
THREE = ((1, 0), (0, 1), (0, 0))


def third(index):
    return (index * 11) >> 5


def kernel(
    wa_count,
    q_hbm,
    k_hbm,
    v_hbm,
    c_hbm,
    dq_ref,
    dk_ref,
    dv_ref,
    kv,
    qc,
    halo,
    packed,
    bias,
    qs,
    cs,
    sheet_out,
    sheet_in,
    terms,
    back,
    part_out,
    part_in,
    load_sem,
    row_sem,
    col_sem,
    sheet_sem,
    term_sem,
    part_sem,
):
    images, tokens, channels = q_hbm.shape
    head_size = channels // HEADS
    ha = lax.axis_index("ha")
    wa = lax.axis_index("wa")
    other = 1 - ha
    has = (wa > 0, wa < wa_count - 1)
    side_device = ((ha, jnp.maximum(wa - 1, 0)), (ha, jnp.minimum(wa + 1, wa_count - 1)))
    partner = (other, wa)

    barrier = pltpu.get_barrier_semaphore()

    def greet(device):
        pl.semaphore_signal(barrier, inc=1, device_id=device, device_id_type=MESH)

    greet(partner)
    for side in range(2):
        pl.when(has[side])(functools.partial(greet, side_device[side]))

    loads = {}
    for name, ref, target in (
        ("k", k_hbm, kv.at[:, 0, pl.ds(0, tokens)]),
        ("v", v_hbm, kv.at[:, 1, pl.ds(0, tokens)]),
        ("q", q_hbm, qc.at[:, 0]),
        ("c", c_hbm, qc.at[:, 1]),
    ):
        loads[name] = pltpu.make_async_copy(ref, target, load_sem.at[len(loads)])
        loads[name].start()

    edge = (TILE - REACH) * other

    def iota(shape, dim):
        return lax.broadcasted_iota(jnp.int32, shape, dim)

    lane = iota((1, LANES), 1)
    slot = jnp.where(lane < OWN, lane & (tokens - 1), lane & (SLOTS - 1))
    own_row = ((slot >> 3) + edge) & (TILE - 1)
    far_row = jnp.where(slot < EDGE, jnp.where(ha == 0, TILE, -REACH) + (slot >> 3), 100)
    query_row = jnp.where(lane < OWN, own_row, far_row)
    query_col = slot & (TILE - 1)
    for first, size in ((0, tokens), (LEFT, EDGE), (RIGHT, EDGE)):
        index = iota((size, 1), 0)
        if first == 0:
            row, col = index >> 3, index & (TILE - 1)
        else:
            row = third(index)
            col = index - 3 * row + (-REACH if first == LEFT else TILE)
            row = row + jnp.where(has[0 if first == LEFT else 1], 0, 1000)
        gap = jnp.maximum(jnp.abs(row - query_row), jnp.abs(col - query_col))
        bias[first : first + size] = jnp.where(gap <= REACH, 0.0, FAR)
    for image in range(images):
        for field in range(2):
            halo[image, field, EDGE:SLOTS] = jnp.zeros((SLOTS - EDGE, channels), jnp.float32)

    def clear(first):
        for image in range(images):
            for field in range(2):
                kv[image, field, first : first + EDGE] = jnp.zeros((EDGE, channels), jnp.float32)

    pl.when(jnp.logical_not(has[0]))(lambda: clear(LEFT))
    pl.when(jnp.logical_not(has[1]))(lambda: clear(RIGHT))

    cut = (slice(0, REACH), slice(TILE - REACH, TILE))
    for field, name in enumerate("kv"):
        loads[name].wait()
        for image in range(images):
            mine = kv[image, field, 0:tokens]
            for row in range(TILE):
                line = mine[row * TILE : (row + 1) * TILE]
                for side in range(2):
                    packed[image, side, field, 3 * row : 3 * row + 3] = line[cut[side]]
    loads["q"].wait()
    loads["c"].wait()

    pl.semaphore_wait(barrier, 1 + has[0].astype(jnp.int32) + has[1].astype(jnp.int32))

    def remote(source, target, sems, index, device):
        return pltpu.make_async_remote_copy(
            src_ref=source,
            dst_ref=target,
            send_sem=sems.at[(0,) + index],
            recv_sem=sems.at[(1,) + index],
            device_id=device,
            device_id_type=MESH,
        )

    edge_start = pl.multiple_of(edge * TILE, TILE)

    def row_copy(image):
        source = qc.at[image, :, pl.ds(edge_start, EDGE)]
        return remote(source, halo.at[image, :, pl.ds(0, EDGE)], row_sem, (image,), partner)

    def col_copy(image, side):
        target = kv.at[image, :, pl.ds((RIGHT, LEFT)[side], EDGE)]
        return remote(packed.at[image, side], target, col_sem, (image, side), side_device[side])

    def sheet_copy(image):
        return remote(sheet_out.at[image], sheet_in.at[image], sheet_sem, (image,), partner)

    def term_copy(image, side):
        source, target = terms.at[image, side], back.at[image, side]
        return remote(source, target, term_sem, (image, side), side_device[side])

    def part_copy(image):
        return remote(part_out.at[image], part_in.at[image], part_sem, (image,), partner)

    for image in range(images):
        row_copy(image).start()
        for side in range(2):
            pl.when(has[side])(col_copy(image, side).start)

    lane_head = iota((tokens, channels), 1) // head_size
    heads = [jnp.where(lane_head == head, 1.0, 0.0).astype(jnp.bfloat16) for head in range(HEADS)]

    def turned(row):
        return pl.ds(pl.multiple_of(((row + edge) & (TILE - 1)) * TILE, TILE), TILE)

    def stack_own(image):
        for field, stack, factor, parts in ((0, qs, SCALE, 3), (1, cs, 1.0, 2)):
            field_rows = [qc[image, field, turned(row)] for row in range(TILE)]
            for index, part in enumerate(split(jnp.concatenate(field_rows, 0) * factor, parts)):
                for head in range(HEADS):
                    stack[image, index, head * tokens : (head + 1) * tokens] = part * heads[head]

    def stack_halo(image):
        for field, stack, factor, parts in ((0, qs, SCALE, 3), (1, cs, 1.0, 2)):
            for index, part in enumerate(split(halo[image, field] * factor, parts)):
                for head in range(HEADS):
                    base = OWN + SLOTS * head
                    stack[image, index, base : base + SLOTS] = part * heads[head][:SLOTS]

    def parts_of(ref, image, count):
        return [ref[image, index] for index in range(count)]

    lane128 = iota((8, 128), 1)

    def to_slots(wide_sheet):
        low, high = wide_sheet[:, :128], wide_sheet[:, 128:]
        out = jnp.where(lane128 < 32, low, pltpu.roll(low, 96, 1))
        out = jnp.where(lane128 < 64, out, pltpu.roll(high, 64, 1))
        return jnp.where(lane128 < 96, out, pltpu.roll(high, 32, 1))

    def from_slots(sheet):
        low = jnp.where(lane128 < 64, sheet, pltpu.roll(sheet, 32, 1))
        high = jnp.where(lane128 < 64, pltpu.roll(sheet, 64, 1), pltpu.roll(sheet, 96, 1))
        return jnp.concatenate([low, high], axis=1)

    def first_pass(image):
        keys = split(kv[image, 0], 3)
        scores = product(keys, parts_of(qs, image, 3), SIX, ((1,), (1,))) + bias[...]
        values = split(kv[image, 1], 2)
        dprobs = product(values, parts_of(cs, image, 2), THREE, ((1,), (1,)))
        top = jnp.max(scores, axis=0, keepdims=True)
        expd = jnp.exp(scores - top)
        mass = jnp.sum(expd, axis=0, keepdims=True)
        moment = jnp.sum(expd * dprobs, axis=0, keepdims=True)
        sheet = jnp.concatenate([top, mass, moment, jnp.zeros((5, LANES), jnp.float32)], axis=0)
        mine = to_slots(sheet[:, :OWN])
        sheet_out[image, 0:3] = mine[0:3]
        sheet_out[image, 3:6] = sheet[0:3, OWN:]
        sheet_out[image, 6:8] = jnp.zeros((2, 128), jnp.float32)
        sheet_copy(image).start()
        return keys, expd, dprobs, top, mass, moment

    def fold(stacked, size):
        total = jnp.zeros((size, channels), jnp.float32)
        for head in range(HEADS):
            total = total + jnp.where(
                lane_head[:size] == head, stacked[head * size : (head + 1) * size], 0.0
            )
        return total

    live_own = (iota((1, OWN), 1) & (tokens - 1)) < EDGE
    live_far = (iota((1, 128), 1) & (SLOTS - 1)) < EDGE

    def second_pass(image, keys, expd, dprobs, top, mass, moment):
        sheet_copy(image).wait_recv()
        sheet = sheet_in[image]
        seen = from_slots(jnp.concatenate([sheet[3:6], jnp.zeros((5, 128), jnp.float32)], 0))
        top_b = jnp.where(live_own, seen[0:1], FAR)
        mass_b = jnp.where(live_own, seen[1:2], 0.0)
        moment_b = jnp.where(live_own, seen[2:3], 0.0)
        top_b = jnp.concatenate([top_b, sheet[0:1]], axis=1)
        mass_b = jnp.concatenate([mass_b, sheet[1:2]], axis=1)
        moment_b = jnp.concatenate([moment_b, sheet[2:3]], axis=1)
        highest = jnp.maximum(top, top_b)
        share_a = jnp.exp(top - highest)
        share_b = jnp.exp(top_b - highest)
        norm = 1.0 / (mass * share_a + mass_b * share_b)
        delta = (moment * share_a + moment_b * share_b) * norm
        factor = share_a * norm
        factor = jnp.concatenate(
            [factor[:, :OWN], jnp.where(live_far, factor[:, OWN:], 0.0)], axis=1
        )
        probs = expd * factor
        dscores = probs * (dprobs - delta)
        dparts = split(dscores, 2)
        dkeys = product(dparts, parts_of(qs, image, 2), THREE, ((1,), (0,)))
        dvalues = product(split(probs, 2), parts_of(cs, image, 2), THREE, ((1,), (0,)))
        for side, first in enumerate((LEFT, RIGHT)):
            terms[image, side, 0] = dkeys[first : first + EDGE]
            terms[image, side, 1] = dvalues[first : first + EDGE]
            pl.when(has[side])(term_copy(image, side).start)
        spread = product(dparts, keys, THREE, ((0,), (0,)))
        part_out[image] = fold(spread[OWN:], SLOTS)[:EDGE] * SCALE
        part_copy(image).start()
        dk_ref[image] = dkeys[:tokens]
        dv_ref[image] = dvalues[:tokens]
        own = fold(spread[:OWN], tokens) * SCALE
        for row in range(TILE):
            dq_ref[image, turned(row)] = own[row * TILE : (row + 1) * TILE]

    for image in range(images):
        stack_own(image)
    kept = []
    for image in range(images):
        row_copy(image).wait_recv()
        stack_halo(image)
        for side in range(2):
            pl.when(has[side])(col_copy(image, 1 - side).wait_recv)
        kept.append(first_pass(image))
    for image in range(images):
        second_pass(image, *kept[image])

    for image in range(images):
        for side in range(2):

            def add(image=image, side=side):
                term_copy(image, 1 - side).wait_recv()
                for field, ref in enumerate((dk_ref, dv_ref)):
                    for row in range(TILE):
                        at = row * TILE + cut[side].start
                        ref[image, at : at + 3] += back[image, 1 - side, field, 3 * row : 3 * row + 3]

            pl.when(has[side])(add)
        part_copy(image).wait_recv()
        dq_ref[image, pl.ds(edge_start, EDGE)] += part_in[image]

    for image in range(images):
        row_copy(image).wait_send()
        sheet_copy(image).wait_send()
        part_copy(image).wait_send()
        for side in range(2):
            pl.when(has[side])(col_copy(image, side).wait_send)
            pl.when(has[side])(term_copy(image, side).wait_send)


def store(*refs):
    sem = refs[6]
    copies = [pltpu.make_async_copy(refs[i], refs[3 + i], sem.at[i]) for i in range(3)]
    for copy in copies:
        copy.start()
    for copy in copies:
        copy.wait()


def per_device(wa_count, queries, keys, values, cotangent):
    images, tile_rows, tile_cols, channels = queries.shape
    flat = (images, tile_rows * tile_cols, channels)
    f32, bf16 = jnp.float32, jnp.bfloat16
    out = jax.ShapeDtypeStruct(flat, f32)
    sems = pltpu.SemaphoreType.DMA
    results = pl.pallas_call(
        functools.partial(kernel, wa_count),
        out_shape=(pltpu.VMEM(flat, f32),) * 3,
        in_specs=[pl.BlockSpec(memory_space=pl.ANY)] * 4,
        out_specs=(pl.BlockSpec(memory_space=pltpu.VMEM),) * 3,
        scratch_shapes=[
            pltpu.VMEM((images, 2, WIDE, channels), f32),
            pltpu.VMEM((images, 2, TOKENS, channels), f32),
            pltpu.VMEM((images, 2, SLOTS, channels), f32),
            pltpu.VMEM((images, 2, 2, EDGE, channels), f32),
            pltpu.VMEM((WIDE, LANES), f32),
            pltpu.VMEM((images, 3, LANES, channels), bf16),
            pltpu.VMEM((images, 2, LANES, channels), bf16),
            pltpu.VMEM((images, 8, 128), f32),
            pltpu.VMEM((images, 8, 128), f32),
            pltpu.VMEM((images, 2, 2, EDGE, channels), f32),
            pltpu.VMEM((images, 2, 2, EDGE, channels), f32),
            pltpu.VMEM((images, EDGE, channels), f32),
            pltpu.VMEM((images, EDGE, channels), f32),
            sems((4,)),
            sems((2, images)),
            sems((2, images, 2)),
            sems((2, images)),
            sems((2, images, 2)),
            sems((2, images)),
        ],
        compiler_params=pltpu.CompilerParams(collective_id=0, has_side_effects=True),
    )(*(x.reshape(flat) for x in (queries, keys, values, cotangent)))
    results = pl.pallas_call(
        store,
        out_shape=(out, out, out),
        in_specs=[pl.BlockSpec(memory_space=pltpu.VMEM)] * 3,
        out_specs=(pl.BlockSpec(memory_space=pl.ANY),) * 3,
        scratch_shapes=[sems((3,))],
    )(*(pltpu.with_memory_space_constraint(x, pltpu.VMEM) for x in results))
    return tuple(x.reshape(queries.shape) for x in results)


def solution(mesh):
    spec = P(None, "ha", "wa", None)
    return jax.shard_map(
        functools.partial(per_device, mesh.shape["wa"]),
        mesh=mesh,
        in_specs=(spec,) * 4,
        out_specs=(spec,) * 3,
        check_vma=False,
    )
```

```python
import functools

import jax
import jax.numpy as jnp
from jax import lax
from jax.experimental import pallas as pl
from jax.experimental.pallas import tpu as pltpu
from jax.sharding import PartitionSpec as P

HEADS = 4
REACH = 3
MESH = pl.DeviceIdType.MESH

TILE = 8
TOKENS = 64
EDGE = REACH * TILE
LEFT = 64
RIGHT = 88
WIDE = 112
OWN = 256
SLOTS = 32
LANES = 384
SCALE = 1.0 / 8.0
FAR = -1e30


def dot(a, b, contract):
    return lax.dot_general(a, b, (contract, ((), ())), preferred_element_type=jnp.float32)


def split(x, parts):
    out = []
    for index in range(parts):
        part = x.astype(jnp.bfloat16)
        out.append(part)
        if index + 1 < parts:
            x = x - part.astype(jnp.float32)
    return out


def beside(parts, order):
    return jnp.concatenate([parts[index] for index in order], axis=1)


def below(parts, order):
    return jnp.concatenate([parts[index] for index in order], axis=0)


def product(a, b, order, contract):
    left = beside if contract[0][0] else below
    right = beside if contract[1][0] else below
    return dot(left(a, [i for i, _ in order]), right(b, [j for _, j in order]), contract)


SIX = ((2, 0), (0, 2), (1, 1), (1, 0), (0, 1), (0, 0))
THREE = ((1, 0), (0, 1), (0, 0))


def third(index):
    return (index * 11) >> 5


def kernel(
    wa_count,
    q_hbm,
    k_hbm,
    v_hbm,
    c_hbm,
    dq_ref,
    dk_ref,
    dv_ref,
    kv,
    qc,
    halo,
    packed,
    bias,
    qs,
    cs,
    sheet_out,
    sheet_in,
    terms,
    back,
    part_out,
    part_in,
    load_sem,
    row_sem,
    col_sem,
    sheet_sem,
    term_sem,
    part_sem,
):
    images, tokens, channels = q_hbm.shape
    head_size = channels // HEADS
    ha = lax.axis_index("ha")
    wa = lax.axis_index("wa")
    other = 1 - ha
    has = (wa > 0, wa < wa_count - 1)
    side_device = ((ha, jnp.maximum(wa - 1, 0)), (ha, jnp.minimum(wa + 1, wa_count - 1)))
    partner = (other, wa)

    barrier = pltpu.get_barrier_semaphore()

    def greet(device):
        pl.semaphore_signal(barrier, inc=1, device_id=device, device_id_type=MESH)

    greet(partner)
    for side in range(2):
        pl.when(has[side])(functools.partial(greet, side_device[side]))

    loads = {}
    for name, ref, target in (
        ("k", k_hbm, kv.at[:, 0, pl.ds(0, tokens)]),
        ("v", v_hbm, kv.at[:, 1, pl.ds(0, tokens)]),
        ("q", q_hbm, qc.at[:, 0]),
        ("c", c_hbm, qc.at[:, 1]),
    ):
        loads[name] = pltpu.make_async_copy(ref, target, load_sem.at[len(loads)])
        loads[name].start()

    edge = (TILE - REACH) * other

    def iota(shape, dim):
        return lax.broadcasted_iota(jnp.int32, shape, dim)

    lane = iota((1, LANES), 1)
    slot = jnp.where(lane < OWN, lane & (tokens - 1), lane & (SLOTS - 1))
    own_row = ((slot >> 3) + edge) & (TILE - 1)
    far_row = jnp.where(slot < EDGE, jnp.where(ha == 0, TILE, -REACH) + (slot >> 3), 100)
    query_row = jnp.where(lane < OWN, own_row, far_row)
    query_col = slot & (TILE - 1)
    for first, size in ((0, tokens), (LEFT, EDGE), (RIGHT, EDGE)):
        index = iota((size, 1), 0)
        if first == 0:
            row, col = index >> 3, index & (TILE - 1)
        else:
            row = third(index)
            col = index - 3 * row + (-REACH if first == LEFT else TILE)
            row = row + jnp.where(has[0 if first == LEFT else 1], 0, 1000)
        gap = jnp.maximum(jnp.abs(row - query_row), jnp.abs(col - query_col))
        bias[first : first + size] = jnp.where(gap <= REACH, 0.0, FAR)
    for image in range(images):
        for field in range(2):
            halo[image, field, EDGE:SLOTS] = jnp.zeros((SLOTS - EDGE, channels), jnp.float32)

    def clear(first):
        for image in range(images):
            for field in range(2):
                kv[image, field, first : first + EDGE] = jnp.zeros((EDGE, channels), jnp.float32)

    pl.when(jnp.logical_not(has[0]))(lambda: clear(LEFT))
    pl.when(jnp.logical_not(has[1]))(lambda: clear(RIGHT))

    cut = (slice(0, REACH), slice(TILE - REACH, TILE))

    def pack():
        for name in "kvqc":
            loads[name].wait()
        for image in range(images):
            for field in range(2):
                mine = kv[image, field, 0:tokens]
                for row in range(TILE):
                    line = mine[row * TILE : (row + 1) * TILE]
                    for side in range(2):
                        packed[image, side, field, 3 * row : 3 * row + 3] = line[cut[side]]

    pack()
    pl.semaphore_wait(barrier, 1 + has[0].astype(jnp.int32) + has[1].astype(jnp.int32))

    def remote(source, target, sems, index, device):
        return pltpu.make_async_remote_copy(
            src_ref=source,
            dst_ref=target,
            send_sem=sems.at[(0,) + index],
            recv_sem=sems.at[(1,) + index],
            device_id=device,
            device_id_type=MESH,
        )

    edge_start = pl.multiple_of(edge * TILE, TILE)

    def row_copy(image):
        source = qc.at[image, :, pl.ds(edge_start, EDGE)]
        return remote(source, halo.at[image, :, pl.ds(0, EDGE)], row_sem, (image,), partner)

    def col_copy(image, side):
        target = kv.at[image, :, pl.ds((RIGHT, LEFT)[side], EDGE)]
        return remote(packed.at[image, side], target, col_sem, (image, side), side_device[side])

    def sheet_copy(image, kind):
        source, target = sheet_out.at[image, kind], sheet_in.at[image, kind]
        return remote(source, target, sheet_sem, (image, kind), partner)

    def term_copy(image, side):
        source, target = terms.at[image, side], back.at[image, side]
        return remote(source, target, term_sem, (image, side), side_device[side])

    def part_copy(image):
        return remote(part_out.at[image], part_in.at[image], part_sem, (image,), partner)

    for image in range(images):
        row_copy(image).start()
        for side in range(2):
            pl.when(has[side])(col_copy(image, side).start)

    lane_head = iota((tokens, channels), 1) // head_size
    heads = [jnp.where(lane_head == head, 1.0, 0.0).astype(jnp.bfloat16) for head in range(HEADS)]

    def turned(row):
        return pl.ds(pl.multiple_of(((row + edge) & (TILE - 1)) * TILE, TILE), TILE)

    def stack_own(image):
        for field, stack, factor, parts in ((0, qs, SCALE, 3), (1, cs, 1.0, 2)):
            field_rows = [qc[image, field, turned(row)] for row in range(TILE)]
            for index, part in enumerate(split(jnp.concatenate(field_rows, 0) * factor, parts)):
                for head in range(HEADS):
                    stack[image, index, head * tokens : (head + 1) * tokens] = part * heads[head]

    def stack_halo(image):
        for field, stack, factor, parts in ((0, qs, SCALE, 3), (1, cs, 1.0, 2)):
            for index, part in enumerate(split(halo[image, field] * factor, parts)):
                for head in range(HEADS):
                    base = OWN + SLOTS * head
                    stack[image, index, base : base + SLOTS] = part * heads[head][:SLOTS]

    lane128 = iota((8, 128), 1)

    def to_slots(wide_sheet):
        low, high = wide_sheet[:, :128], wide_sheet[:, 128:]
        out = jnp.where(lane128 < 32, low, pltpu.roll(low, 96, 1))
        out = jnp.where(lane128 < 64, out, pltpu.roll(high, 64, 1))
        return jnp.where(lane128 < 96, out, pltpu.roll(high, 32, 1))

    def from_slots(sheet):
        low = jnp.where(lane128 < 64, sheet, pltpu.roll(sheet, 32, 1))
        high = jnp.where(lane128 < 64, pltpu.roll(sheet, 64, 1), pltpu.roll(sheet, 96, 1))
        return jnp.concatenate([low, high], axis=1)

    def first_pass(image, first, size, keys, values):
        lanes = slice(first, first + size)
        stacked = [qs[image, index, lanes] for index in range(3)]
        scores = product(keys, stacked, SIX, ((1,), (1,))) + bias[:, lanes]
        stacked = [cs[image, index, lanes] for index in range(2)]
        dprobs = product(values, stacked, THREE, ((1,), (1,)))
        top = jnp.max(scores, axis=0, keepdims=True)
        expd = jnp.exp(scores - top)
        mass = jnp.sum(expd, axis=0, keepdims=True)
        moment = jnp.sum(expd * dprobs, axis=0, keepdims=True)
        sheet = jnp.concatenate([top, mass, moment, jnp.zeros((5, size), jnp.float32)], axis=0)
        kind = int(first == OWN)
        sheet_out[image, kind] = sheet if kind else to_slots(sheet)
        sheet_copy(image, kind).start()
        return expd, dprobs, top, mass, moment

    def fold(stacked, size):
        total = jnp.zeros((size, channels), jnp.float32)
        for head in range(HEADS):
            total = total + jnp.where(
                lane_head[:size] == head, stacked[head * size : (head + 1) * size], 0.0
            )
        return total

    live_own = (iota((1, OWN), 1) & (tokens - 1)) < EDGE
    live_far = (iota((1, 128), 1) & (SLOTS - 1)) < EDGE

    def weights(image, first, size, expd, dprobs, top, mass, moment):
        kind = int(first != OWN)
        sheet_copy(image, kind).wait_recv()
        sheet = sheet_in[image, kind]
        if kind:
            sheet = from_slots(sheet)
            top_b = jnp.where(live_own, sheet[0:1], FAR)
            mass_b = jnp.where(live_own, sheet[1:2], 0.0)
            moment_b = jnp.where(live_own, sheet[2:3], 0.0)
        else:
            top_b, mass_b, moment_b = sheet[0:1], sheet[1:2], sheet[2:3]
        highest = jnp.maximum(top, top_b)
        share_a = jnp.exp(top - highest)
        share_b = jnp.exp(top_b - highest)
        norm = 1.0 / (mass * share_a + mass_b * share_b)
        delta = (moment * share_a + moment_b * share_b) * norm
        factor = share_a * norm
        if not kind:
            factor = jnp.where(live_far, factor, 0.0)
        probs = expd * factor
        dscores = probs * (dprobs - delta)
        return split(probs, 2), split(dscores, 2)

    def key_terms(image, first, size, probs, dscores):
        lanes = slice(first, first + size)
        stacked = [qs[image, index, lanes] for index in range(2)]
        dkeys = product(dscores, stacked, THREE, ((1,), (0,)))
        stacked = [cs[image, index, lanes] for index in range(2)]
        return dkeys, product(probs, stacked, THREE, ((1,), (0,)))

    for image in range(images):
        stack_own(image)
    parts, own_kept, far_kept, far_terms, own_grads = [], [], [], [], []
    for image in range(images):
        for side in range(2):
            pl.when(has[side])(col_copy(image, 1 - side).wait_recv)
        parts.append((split(kv[image, 0], 3), split(kv[image, 1], 2)))
        own_kept.append(first_pass(image, 0, OWN, *parts[image]))
    for image in range(images):
        row_copy(image).wait_recv()
        stack_halo(image)
        far_kept.append(first_pass(image, OWN, LANES - OWN, *parts[image]))
    for image in range(images):
        far_kept[image] = weights(image, OWN, LANES - OWN, *far_kept[image])
        spread = product(far_kept[image][1], parts[image][0], THREE, ((0,), (0,)))
        part_out[image] = fold(spread, SLOTS)[:EDGE] * SCALE
        part_copy(image).start()
    for image in range(images):
        far_terms.append(key_terms(image, OWN, LANES - OWN, *far_kept[image]))
    for image in range(images):
        own_kept[image] = weights(image, 0, OWN, *own_kept[image])
        dkeys, dvalues = key_terms(image, 0, OWN, *own_kept[image])
        dkeys = dkeys + far_terms[image][0]
        dvalues = dvalues + far_terms[image][1]
        for side, first in enumerate((LEFT, RIGHT)):
            terms[image, side, 0] = dkeys[first : first + EDGE]
            terms[image, side, 1] = dvalues[first : first + EDGE]
            pl.when(has[side])(term_copy(image, side).start)
        own_grads.append((dkeys[:tokens], dvalues[:tokens]))
    for image in range(images):
        dk_ref[image], dv_ref[image] = own_grads[image]
        spread = product(own_kept[image][1], parts[image][0], THREE, ((0,), (0,)))
        own = fold(spread, tokens) * SCALE
        for row in range(TILE):
            dq_ref[image, turned(row)] = own[row * TILE : (row + 1) * TILE]

    for image in range(images):
        for side in range(2):

            def add(image=image, side=side):
                term_copy(image, 1 - side).wait_recv()
                for field, ref in enumerate((dk_ref, dv_ref)):
                    for row in range(TILE):
                        at = row * TILE + cut[side].start
                        ref[image, at : at + 3] += back[image, 1 - side, field, 3 * row : 3 * row + 3]

            pl.when(has[side])(add)
        part_copy(image).wait_recv()
        dq_ref[image, pl.ds(edge_start, EDGE)] += part_in[image]

    for image in range(images):
        row_copy(image).wait_send()
        for kind in range(2):
            sheet_copy(image, kind).wait_send()
        part_copy(image).wait_send()
        for side in range(2):
            pl.when(has[side])(col_copy(image, side).wait_send)
            pl.when(has[side])(term_copy(image, side).wait_send)


def store(*refs):
    sem = refs[6]
    copies = [pltpu.make_async_copy(refs[i], refs[3 + i], sem.at[i]) for i in range(3)]
    for copy in copies:
        copy.start()
    for copy in copies:
        copy.wait()


def per_device(wa_count, queries, keys, values, cotangent):
    images, tile_rows, tile_cols, channels = queries.shape
    flat = (images, tile_rows * tile_cols, channels)
    f32, bf16 = jnp.float32, jnp.bfloat16
    out = jax.ShapeDtypeStruct(flat, f32)
    sems = pltpu.SemaphoreType.DMA
    results = pl.pallas_call(
        functools.partial(kernel, wa_count),
        out_shape=(pltpu.VMEM(flat, f32),) * 3,
        in_specs=[pl.BlockSpec(memory_space=pl.ANY)] * 4,
        out_specs=(pl.BlockSpec(memory_space=pltpu.VMEM),) * 3,
        scratch_shapes=[
            pltpu.VMEM((images, 2, WIDE, channels), f32),
            pltpu.VMEM((images, 2, TOKENS, channels), f32),
            pltpu.VMEM((images, 2, SLOTS, channels), f32),
            pltpu.VMEM((images, 2, 2, EDGE, channels), f32),
            pltpu.VMEM((WIDE, LANES), f32),
            pltpu.VMEM((images, 3, LANES, channels), bf16),
            pltpu.VMEM((images, 2, LANES, channels), bf16),
            pltpu.VMEM((images, 2, 8, 128), f32),
            pltpu.VMEM((images, 2, 8, 128), f32),
            pltpu.VMEM((images, 2, 2, EDGE, channels), f32),
            pltpu.VMEM((images, 2, 2, EDGE, channels), f32),
            pltpu.VMEM((images, EDGE, channels), f32),
            pltpu.VMEM((images, EDGE, channels), f32),
            sems((4,)),
            sems((2, images)),
            sems((2, images, 2)),
            sems((2, images, 2)),
            sems((2, images, 2)),
            sems((2, images)),
        ],
        compiler_params=pltpu.CompilerParams(collective_id=0, has_side_effects=True),
    )(*(x.reshape(flat) for x in (queries, keys, values, cotangent)))
    results = pl.pallas_call(
        store,
        out_shape=(out, out, out),
        in_specs=[pl.BlockSpec(memory_space=pltpu.VMEM)] * 3,
        out_specs=(pl.BlockSpec(memory_space=pl.ANY),) * 3,
        scratch_shapes=[sems((3,))],
    )(*(pltpu.with_memory_space_constraint(x, pltpu.VMEM) for x in results))
    return tuple(x.reshape(queries.shape) for x in results)


def solution(mesh):
    spec = P(None, "ha", "wa", None)
    return jax.shard_map(
        functools.partial(per_device, mesh.shape["wa"]),
        mesh=mesh,
        in_specs=(spec,) * 4,
        out_specs=(spec,) * 3,
        check_vma=False,
    )
```

```python
import functools

import jax
import jax.numpy as jnp
from jax import lax
from jax.experimental import pallas as pl
from jax.experimental.pallas import tpu as pltpu
from jax.sharding import PartitionSpec as P

HEADS = 4
REACH = 3
MESH = pl.DeviceIdType.MESH

TILE = 8
TOKENS = 64
EDGE = REACH * TILE
LEFT = 64
RIGHT = 88
WIDE = 112
OWN = 256
SLOTS = 32
LANES = 384
SCALE = 1.0 / 8.0
FAR = -1e30


def dot(a, b, contract):
    return lax.dot_general(a, b, (contract, ((), ())), preferred_element_type=jnp.float32)


def split(x, parts):
    out = []
    for index in range(parts):
        part = x.astype(jnp.bfloat16)
        out.append(part)
        if index + 1 < parts:
            x = x - part.astype(jnp.float32)
    return out


def beside(parts, order):
    return jnp.concatenate([parts[index] for index in order], axis=1)


def below(parts, order):
    return jnp.concatenate([parts[index] for index in order], axis=0)


def product(a, b, order, contract):
    left = beside if contract[0][0] else below
    right = beside if contract[1][0] else below
    return dot(left(a, [i for i, _ in order]), right(b, [j for _, j in order]), contract)


SIX = ((2, 0), (0, 2), (1, 1), (1, 0), (0, 1), (0, 0))
THREE = ((1, 0), (0, 1), (0, 0))


def third(index):
    return (index * 11) >> 5


def kernel(
    wa_count,
    q_hbm,
    k_hbm,
    v_hbm,
    c_hbm,
    dq_ref,
    dk_ref,
    dv_ref,
    kv,
    qc,
    halo,
    packed,
    bias,
    qs,
    cs,
    qt,
    ct,
    sheet_out,
    sheet_in,
    terms,
    back,
    part_out,
    part_in,
    load_sem,
    row_sem,
    col_sem,
    sheet_sem,
    term_sem,
    part_sem,
):
    images, tokens, channels = q_hbm.shape
    head_size = channels // HEADS
    ha = lax.axis_index("ha")
    wa = lax.axis_index("wa")
    other = 1 - ha
    has = (wa > 0, wa < wa_count - 1)
    side_device = ((ha, jnp.maximum(wa - 1, 0)), (ha, jnp.minimum(wa + 1, wa_count - 1)))
    partner = (other, wa)

    barrier = pltpu.get_barrier_semaphore()

    def greet(device):
        pl.semaphore_signal(barrier, inc=1, device_id=device, device_id_type=MESH)

    greet(partner)
    for side in range(2):
        pl.when(has[side])(functools.partial(greet, side_device[side]))

    loads = {}
    for name, ref, target in (
        ("k", k_hbm, kv.at[:, 0, pl.ds(0, tokens)]),
        ("v", v_hbm, kv.at[:, 1, pl.ds(0, tokens)]),
        ("q", q_hbm, qc.at[:, 0]),
        ("c", c_hbm, qc.at[:, 1]),
    ):
        loads[name] = pltpu.make_async_copy(ref, target, load_sem.at[len(loads)])
        loads[name].start()

    edge = (TILE - REACH) * other

    def iota(shape, dim):
        return lax.broadcasted_iota(jnp.int32, shape, dim)

    lane = iota((1, LANES), 1)
    slot = jnp.where(lane < OWN, lane & (tokens - 1), lane & (SLOTS - 1))
    own_row = ((slot >> 3) + edge) & (TILE - 1)
    far_row = jnp.where(slot < EDGE, jnp.where(ha == 0, TILE, -REACH) + (slot >> 3), 100)
    query_row = jnp.where(lane < OWN, own_row, far_row)
    query_col = slot & (TILE - 1)
    for first, size in ((0, tokens), (LEFT, EDGE), (RIGHT, EDGE)):
        index = iota((size, 1), 0)
        if first == 0:
            row, col = index >> 3, index & (TILE - 1)
        else:
            row = third(index)
            col = index - 3 * row + (-REACH if first == LEFT else TILE)
            row = row + jnp.where(has[0 if first == LEFT else 1], 0, 1000)
        gap = jnp.maximum(jnp.abs(row - query_row), jnp.abs(col - query_col))
        bias[first : first + size] = jnp.where(gap <= REACH, 0.0, FAR)
    for image in range(images):
        for field in range(2):
            halo[image, field, EDGE:SLOTS] = jnp.zeros((SLOTS - EDGE, channels), jnp.float32)

    def clear(first):
        for image in range(images):
            for field in range(2):
                kv[image, field, first : first + EDGE] = jnp.zeros((EDGE, channels), jnp.float32)

    pl.when(jnp.logical_not(has[0]))(lambda: clear(LEFT))
    pl.when(jnp.logical_not(has[1]))(lambda: clear(RIGHT))

    cut = (slice(0, REACH), slice(TILE - REACH, TILE))

    def pack():
        for name in "kvqc":
            loads[name].wait()
        for image in range(images):
            for field in range(2):
                mine = kv[image, field, 0:tokens]
                for row in range(TILE):
                    line = mine[row * TILE : (row + 1) * TILE]
                    for side in range(2):
                        packed[image, side, field, 3 * row : 3 * row + 3] = line[cut[side]]

    pack()
    pl.semaphore_wait(barrier, 1 + has[0].astype(jnp.int32) + has[1].astype(jnp.int32))

    def remote(source, target, sems, index, device):
        return pltpu.make_async_remote_copy(
            src_ref=source,
            dst_ref=target,
            send_sem=sems.at[(0,) + index],
            recv_sem=sems.at[(1,) + index],
            device_id=device,
            device_id_type=MESH,
        )

    edge_start = pl.multiple_of(edge * TILE, TILE)

    def row_copy(image):
        source = qc.at[image, :, pl.ds(edge_start, EDGE)]
        return remote(source, halo.at[image, :, pl.ds(0, EDGE)], row_sem, (image,), partner)

    def col_copy(image, side):
        target = kv.at[image, :, pl.ds((RIGHT, LEFT)[side], EDGE)]
        return remote(packed.at[image, side], target, col_sem, (image, side), side_device[side])

    def sheet_copy(image, kind):
        source, target = sheet_out.at[image, kind], sheet_in.at[image, kind]
        return remote(source, target, sheet_sem, (image, kind), partner)

    def term_copy(image, side):
        source, target = terms.at[image, side], back.at[image, side]
        return remote(source, target, term_sem, (image, side), side_device[side])

    def part_copy(image):
        return remote(part_out.at[image], part_in.at[image], part_sem, (image,), partner)

    for image in range(images):
        row_copy(image).start()
        for side in range(2):
            pl.when(has[side])(col_copy(image, side).start)

    lane_head = iota((tokens, channels), 1) // head_size
    heads = [jnp.where(lane_head == head, 1.0, 0.0).astype(jnp.bfloat16) for head in range(HEADS)]

    def turned(row):
        return pl.ds(pl.multiple_of(((row + edge) & (TILE - 1)) * TILE, TILE), TILE)

    def stack(image, first, blocks):
        for x, rows, columns, count in ((blocks[0] * SCALE, qs, qt, 3), (blocks[1], cs, ct, 2)):
            size = x.shape[0]
            lanes = slice(first, first + HEADS * size)
            for index, part in enumerate(split(x, 2)):
                for head in range(HEADS):
                    base = first + head * size
                    rows[image, index, base : base + size] = part * heads[head][:size]
            spread = [jnp.where(lane_head[:size] == head, x, 0.0) for head in range(HEADS)]
            turned_x = jnp.transpose(jnp.concatenate(spread, axis=0))
            for index, part in enumerate(split(turned_x, count)):
                columns[image, index, :, lanes] = part

    def stack_own(image):
        stack(
            image,
            0,
            [
                jnp.concatenate([qc[image, field, turned(row)] for row in range(TILE)], axis=0)
                for field in range(2)
            ],
        )

    def stack_halo(image):
        stack(image, OWN, [halo[image, field] for field in range(2)])

    lane128 = iota((8, 128), 1)

    def to_slots(wide_sheet):
        low, high = wide_sheet[:, :128], wide_sheet[:, 128:]
        out = jnp.where(lane128 < 32, low, pltpu.roll(low, 96, 1))
        out = jnp.where(lane128 < 64, out, pltpu.roll(high, 64, 1))
        return jnp.where(lane128 < 96, out, pltpu.roll(high, 32, 1))

    def from_slots(sheet):
        low = jnp.where(lane128 < 64, sheet, pltpu.roll(sheet, 32, 1))
        high = jnp.where(lane128 < 64, pltpu.roll(sheet, 64, 1), pltpu.roll(sheet, 96, 1))
        return jnp.concatenate([low, high], axis=1)

    def first_pass(image, first, size, keys, values):
        lanes = slice(first, first + size)
        stacked = [qt[image, index, :, lanes] for index in range(3)]
        scores = product(keys, stacked, SIX, ((1,), (0,))) + bias[:, lanes]
        stacked = [ct[image, index, :, lanes] for index in range(2)]
        dprobs = product(values, stacked, THREE, ((1,), (0,)))
        top = jnp.max(scores, axis=0, keepdims=True)
        expd = jnp.exp(scores - top)
        mass = jnp.sum(expd, axis=0, keepdims=True)
        moment = jnp.sum(expd * dprobs, axis=0, keepdims=True)
        sheet = jnp.concatenate([top, mass, moment, jnp.zeros((5, size), jnp.float32)], axis=0)
        kind = int(first == OWN)
        sheet_out[image, kind] = sheet if kind else to_slots(sheet)
        sheet_copy(image, kind).start()
        return expd, dprobs, top, mass, moment

    def fold(stacked, size):
        total = jnp.zeros((size, channels), jnp.float32)
        for head in range(HEADS):
            total = total + jnp.where(
                lane_head[:size] == head, stacked[head * size : (head + 1) * size], 0.0
            )
        return total

    live_own = (iota((1, OWN), 1) & (tokens - 1)) < EDGE
    live_far = (iota((1, 128), 1) & (SLOTS - 1)) < EDGE

    def weights(image, first, size, expd, dprobs, top, mass, moment):
        kind = int(first != OWN)
        sheet_copy(image, kind).wait_recv()
        sheet = sheet_in[image, kind]
        if kind:
            sheet = from_slots(sheet)
            top_b = jnp.where(live_own, sheet[0:1], FAR)
            mass_b = jnp.where(live_own, sheet[1:2], 0.0)
            moment_b = jnp.where(live_own, sheet[2:3], 0.0)
        else:
            top_b, mass_b, moment_b = sheet[0:1], sheet[1:2], sheet[2:3]
        highest = jnp.maximum(top, top_b)
        share_a = jnp.exp(top - highest)
        share_b = jnp.exp(top_b - highest)
        norm = 1.0 / (mass * share_a + mass_b * share_b)
        delta = (moment * share_a + moment_b * share_b) * norm
        factor = share_a * norm
        if not kind:
            factor = jnp.where(live_far, factor, 0.0)
        probs = expd * factor
        dscores = probs * (dprobs - delta)
        return split(probs, 2), split(dscores, 2)

    def key_terms(image, first, size, probs, dscores):
        lanes = slice(first, first + size)
        stacked = [qs[image, index, lanes] for index in range(2)]
        dkeys = product(dscores, stacked, THREE, ((1,), (0,)))
        stacked = [cs[image, index, lanes] for index in range(2)]
        return dkeys, product(probs, stacked, THREE, ((1,), (0,)))

    for image in range(images):
        stack_own(image)
    parts, own_kept, far_kept, far_terms, own_grads = [], [], [], [], []
    for image in range(images):
        for side in range(2):
            pl.when(has[side])(col_copy(image, 1 - side).wait_recv)
        parts.append((split(kv[image, 0], 3), split(kv[image, 1], 2)))
        own_kept.append(first_pass(image, 0, OWN, *parts[image]))
    for image in range(images):
        row_copy(image).wait_recv()
        stack_halo(image)
        far_kept.append(first_pass(image, OWN, LANES - OWN, *parts[image]))
    for image in range(images):
        far_kept[image] = weights(image, OWN, LANES - OWN, *far_kept[image])
        spread = product(far_kept[image][1], parts[image][0], THREE, ((0,), (0,)))
        part_out[image] = fold(spread, SLOTS)[:EDGE] * SCALE
        part_copy(image).start()
    for image in range(images):
        far_terms.append(key_terms(image, OWN, LANES - OWN, *far_kept[image]))
    for image in range(images):
        own_kept[image] = weights(image, 0, OWN, *own_kept[image])
        dkeys, dvalues = key_terms(image, 0, OWN, *own_kept[image])
        dkeys = dkeys + far_terms[image][0]
        dvalues = dvalues + far_terms[image][1]
        for side, first in enumerate((LEFT, RIGHT)):
            terms[image, side, 0] = dkeys[first : first + EDGE]
            terms[image, side, 1] = dvalues[first : first + EDGE]
            pl.when(has[side])(term_copy(image, side).start)
        own_grads.append((dkeys[:tokens], dvalues[:tokens]))
    for image in range(images):
        dk_ref[image], dv_ref[image] = own_grads[image]
        spread = product(own_kept[image][1], parts[image][0], THREE, ((0,), (0,)))
        own = fold(spread, tokens) * SCALE
        for row in range(TILE):
            dq_ref[image, turned(row)] = own[row * TILE : (row + 1) * TILE]

    def add(image, side):
        term_copy(image, 1 - side).wait_recv()
        for field, ref in enumerate((dk_ref, dv_ref)):
            for row in range(TILE):
                at = row * TILE + cut[side].start
                ref[image, at : at + 3] += back[image, 1 - side, field, 3 * row : 3 * row + 3]

    for image in range(images):
        part_copy(image).wait_recv()
        dq_ref[image, pl.ds(edge_start, EDGE)] += part_in[image]
    even = lax.rem(wa, 2) == 0
    for parity, order in ((even, (1, 0)), (jnp.logical_not(even), (0, 1))):
        for side in order:
            for image in range(images):
                pl.when(jnp.logical_and(has[side], parity))(functools.partial(add, image, side))

    for image in range(images):
        row_copy(image).wait_send()
        for kind in range(2):
            sheet_copy(image, kind).wait_send()
        part_copy(image).wait_send()
        for side in range(2):
            pl.when(has[side])(col_copy(image, side).wait_send)
            pl.when(has[side])(term_copy(image, side).wait_send)


def store(*refs):
    sem = refs[6]
    copies = [pltpu.make_async_copy(refs[i], refs[3 + i], sem.at[i]) for i in range(3)]
    for copy in copies:
        copy.start()
    for copy in copies:
        copy.wait()


def per_device(wa_count, queries, keys, values, cotangent):
    images, tile_rows, tile_cols, channels = queries.shape
    flat = (images, tile_rows * tile_cols, channels)
    f32, bf16 = jnp.float32, jnp.bfloat16
    out = jax.ShapeDtypeStruct(flat, f32)
    sems = pltpu.SemaphoreType.DMA
    results = pl.pallas_call(
        functools.partial(kernel, wa_count),
        out_shape=(pltpu.VMEM(flat, f32),) * 3,
        in_specs=[pl.BlockSpec(memory_space=pl.ANY)] * 4,
        out_specs=(pl.BlockSpec(memory_space=pltpu.VMEM),) * 3,
        scratch_shapes=[
            pltpu.VMEM((images, 2, WIDE, channels), f32),
            pltpu.VMEM((images, 2, TOKENS, channels), f32),
            pltpu.VMEM((images, 2, SLOTS, channels), f32),
            pltpu.VMEM((images, 2, 2, EDGE, channels), f32),
            pltpu.VMEM((WIDE, LANES), f32),
            pltpu.VMEM((images, 2, LANES, channels), bf16),
            pltpu.VMEM((images, 2, LANES, channels), bf16),
            pltpu.VMEM((images, 3, channels, LANES), bf16),
            pltpu.VMEM((images, 2, channels, LANES), bf16),
            pltpu.VMEM((images, 2, 8, 128), f32),
            pltpu.VMEM((images, 2, 8, 128), f32),
            pltpu.VMEM((images, 2, 2, EDGE, channels), f32),
            pltpu.VMEM((images, 2, 2, EDGE, channels), f32),
            pltpu.VMEM((images, EDGE, channels), f32),
            pltpu.VMEM((images, EDGE, channels), f32),
            sems((4,)),
            sems((2, images)),
            sems((2, images, 2)),
            sems((2, images, 2)),
            sems((2, images, 2)),
            sems((2, images)),
        ],
        compiler_params=pltpu.CompilerParams(collective_id=0, has_side_effects=True),
    )(*(x.reshape(flat) for x in (queries, keys, values, cotangent)))
    results = pl.pallas_call(
        store,
        out_shape=(out, out, out),
        in_specs=[pl.BlockSpec(memory_space=pltpu.VMEM)] * 3,
        out_specs=(pl.BlockSpec(memory_space=pl.ANY),) * 3,
        scratch_shapes=[sems((3,))],
    )(*(pltpu.with_memory_space_constraint(x, pltpu.VMEM) for x in results))
    return tuple(x.reshape(queries.shape) for x in results)


def solution(mesh):
    spec = P(None, "ha", "wa", None)
    return jax.shard_map(
        functools.partial(per_device, mesh.shape["wa"]),
        mesh=mesh,
        in_specs=(spec,) * 4,
        out_specs=(spec,) * 3,
        check_vma=False,
    )
```

```python
import functools

import jax
import jax.numpy as jnp
from jax import lax
from jax.experimental import pallas as pl
from jax.experimental.pallas import tpu as pltpu
from jax.sharding import PartitionSpec as P

HEADS = 4
REACH = 3
MESH = pl.DeviceIdType.MESH

TILE = 8
TOKENS = 64
EDGE = REACH * TILE
LEFT = 64
RIGHT = 88
WIDE = 112
OWN = 256
HALF = 128
SLOTS = 32
LANES = 384
SCALE = 1.0 / 8.0
FAR = -1e30


def dot(a, b, contract):
    return lax.dot_general(a, b, (contract, ((), ())), preferred_element_type=jnp.float32)


def split(x, parts):
    out = []
    for index in range(parts):
        part = x.astype(jnp.bfloat16)
        out.append(part)
        if index + 1 < parts:
            x = x - part.astype(jnp.float32)
    return out


def beside(parts, order):
    return jnp.concatenate([parts[index] for index in order], axis=1)


def below(parts, order):
    return jnp.concatenate([parts[index] for index in order], axis=0)


def product(a, b, order, contract):
    left = beside if contract[0][0] else below
    right = beside if contract[1][0] else below
    return dot(left(a, [i for i, _ in order]), right(b, [j for _, j in order]), contract)


SIX = ((2, 0), (0, 2), (1, 1), (1, 0), (0, 1), (0, 0))
THREE = ((1, 0), (0, 1), (0, 0))


def third(index):
    return (index * 11) >> 5


def kernel(
    wa_count,
    q_hbm,
    k_hbm,
    v_hbm,
    c_hbm,
    dq_ref,
    dk_ref,
    dv_ref,
    kv,
    qc,
    halo,
    packed,
    bias,
    qs,
    cs,
    qt,
    ct,
    sheet_out,
    sheet_in,
    terms,
    back,
    part_out,
    part_in,
    load_sem,
    row_sem,
    col_sem,
    sheet_sem,
    term_sem,
    part_sem,
):
    images, tokens, channels = q_hbm.shape
    head_size = channels // HEADS
    ha = lax.axis_index("ha")
    wa = lax.axis_index("wa")
    other = 1 - ha
    has = (wa > 0, wa < wa_count - 1)
    side_device = ((ha, jnp.maximum(wa - 1, 0)), (ha, jnp.minimum(wa + 1, wa_count - 1)))
    partner = (other, wa)

    barrier = pltpu.get_barrier_semaphore()

    def greet(device):
        pl.semaphore_signal(barrier, inc=1, device_id=device, device_id_type=MESH)

    greet(partner)
    for side in range(2):
        pl.when(has[side])(functools.partial(greet, side_device[side]))

    loads = {}
    for name, ref, target in (
        ("k", k_hbm, kv.at[:, 0, pl.ds(0, tokens)]),
        ("v", v_hbm, kv.at[:, 1, pl.ds(0, tokens)]),
        ("q", q_hbm, qc.at[:, 0]),
        ("c", c_hbm, qc.at[:, 1]),
    ):
        loads[name] = pltpu.make_async_copy(ref, target, load_sem.at[len(loads)])
        loads[name].start()

    edge = (TILE - REACH) * other

    def iota(shape, dim):
        return lax.broadcasted_iota(jnp.int32, shape, dim)

    lane = iota((1, LANES), 1)
    slot = lane & (SLOTS - 1)
    slot = jnp.where((lane >= HALF) & (lane < OWN), slot + SLOTS, slot)
    own_row = ((slot >> 3) + edge) & (TILE - 1)
    far_row = jnp.where(slot < EDGE, jnp.where(ha == 0, TILE, -REACH) + (slot >> 3), 100)
    query_row = jnp.where(lane < OWN, own_row, far_row)
    query_col = slot & (TILE - 1)
    for first, size in ((0, tokens), (LEFT, EDGE), (RIGHT, EDGE)):
        index = iota((size, 1), 0)
        if first == 0:
            row, col = index >> 3, index & (TILE - 1)
        else:
            row = third(index)
            col = index - 3 * row + (-REACH if first == LEFT else TILE)
            row = row + jnp.where(has[0 if first == LEFT else 1], 0, 1000)
        gap = jnp.maximum(jnp.abs(row - query_row), jnp.abs(col - query_col))
        bias[first : first + size] = jnp.where(gap <= REACH, 0.0, FAR)
    for image in range(images):
        for field in range(2):
            halo[image, field, EDGE:SLOTS] = jnp.zeros((SLOTS - EDGE, channels), jnp.float32)

    def clear(first):
        for image in range(images):
            for field in range(2):
                kv[image, field, first : first + EDGE] = jnp.zeros((EDGE, channels), jnp.float32)

    pl.when(jnp.logical_not(has[0]))(lambda: clear(LEFT))
    pl.when(jnp.logical_not(has[1]))(lambda: clear(RIGHT))

    cut = (slice(0, REACH), slice(TILE - REACH, TILE))

    def pack():
        for name in "kvqc":
            loads[name].wait()
        for image in range(images):
            for field in range(2):
                mine = kv[image, field, 0:tokens]
                for row in range(TILE):
                    line = mine[row * TILE : (row + 1) * TILE]
                    for side in range(2):
                        packed[image, side, field, 3 * row : 3 * row + 3] = line[cut[side]]

    pack()
    pl.semaphore_wait(barrier, 1 + has[0].astype(jnp.int32) + has[1].astype(jnp.int32))

    def remote(source, target, sems, index, device):
        return pltpu.make_async_remote_copy(
            src_ref=source,
            dst_ref=target,
            send_sem=sems.at[(0,) + index],
            recv_sem=sems.at[(1,) + index],
            device_id=device,
            device_id_type=MESH,
        )

    edge_start = pl.multiple_of(edge * TILE, TILE)

    def row_copy(image):
        source = qc.at[image, :, pl.ds(edge_start, EDGE)]
        return remote(source, halo.at[image, :, pl.ds(0, EDGE)], row_sem, (image,), partner)

    def col_copy(image, side):
        target = kv.at[image, :, pl.ds((RIGHT, LEFT)[side], EDGE)]
        return remote(packed.at[image, side], target, col_sem, (image, side), side_device[side])

    def sheet_copy(image, kind):
        source, target = sheet_out.at[image, kind], sheet_in.at[image, kind]
        return remote(source, target, sheet_sem, (image, kind), partner)

    def term_copy(image, side):
        source, target = terms.at[image, side], back.at[image, side]
        return remote(source, target, term_sem, (image, side), side_device[side])

    def part_copy(image):
        return remote(part_out.at[image], part_in.at[image], part_sem, (image,), partner)

    for image in range(images):
        row_copy(image).start()
        for side in range(2):
            pl.when(has[side])(col_copy(image, side).start)

    lane_head = iota((tokens, channels), 1) // head_size
    heads = [jnp.where(lane_head == head, 1.0, 0.0).astype(jnp.bfloat16) for head in range(HEADS)]

    def turned(row):
        return pl.ds(pl.multiple_of(((row + edge) & (TILE - 1)) * TILE, TILE), TILE)

    def stack(image, first, blocks):
        for x, rows, columns, count in ((blocks[0] * SCALE, qs, qt, 3), (blocks[1], cs, ct, 2)):
            size = x.shape[0]
            lanes = slice(first, first + HEADS * size)
            for index, part in enumerate(split(x, 2)):
                for head in range(HEADS):
                    base = first + head * size
                    rows[image, index, base : base + size] = part * heads[head][:size]
            spread = [jnp.where(lane_head[:size] == head, x, 0.0) for head in range(HEADS)]
            turned_x = jnp.transpose(jnp.concatenate(spread, axis=0))
            for index, part in enumerate(split(turned_x, count)):
                columns[image, index, :, lanes] = part

    def stack_own(image):
        for half in range(2):
            lines = range(half * SLOTS // TILE, (half + 1) * SLOTS // TILE)
            blocks = [
                jnp.concatenate([qc[image, field, turned(row)] for row in lines], axis=0)
                for field in range(2)
            ]
            stack(image, half * HALF, blocks)

    def stack_halo(image):
        stack(image, OWN, [halo[image, field] for field in range(2)])

    def first_pass(image, first, size, keys, values):
        lanes = slice(first, first + size)
        stacked = [qt[image, index, :, lanes] for index in range(3)]
        scores = product(keys, stacked, SIX, ((1,), (0,))) + bias[:, lanes]
        stacked = [ct[image, index, :, lanes] for index in range(2)]
        dprobs = product(values, stacked, THREE, ((1,), (0,)))
        top = jnp.max(scores, axis=0, keepdims=True)
        expd = jnp.exp(scores - top)
        mass = jnp.sum(expd, axis=0, keepdims=True)
        moment = jnp.sum(expd * dprobs, axis=0, keepdims=True)
        sheet = jnp.concatenate([top, mass, moment, jnp.zeros((5, size), jnp.float32)], axis=0)
        if first != HALF:
            kind = int(first == OWN)
            sheet_out[image, kind] = sheet
            sheet_copy(image, kind).start()
        return expd, dprobs, top, mass, moment

    def fold(stacked, size):
        total = jnp.zeros((size, channels), jnp.float32)
        for head in range(HEADS):
            total = total + jnp.where(
                lane_head[:size] == head, stacked[head * size : (head + 1) * size], 0.0
            )
        return total

    live_far = (iota((1, 128), 1) & (SLOTS - 1)) < EDGE

    def weights(image, first, size, expd, dprobs, top, mass, moment):
        kind = int(first != OWN)
        sheet_copy(image, kind).wait_recv()
        sheet = sheet_in[image, kind]
        top_b, mass_b, moment_b = sheet[0:1], sheet[1:2], sheet[2:3]
        if kind:
            blank = jnp.zeros((1, HALF), jnp.float32)
            top_b = jnp.concatenate([jnp.where(live_far, top_b, FAR), blank + FAR], axis=1)
            mass_b = jnp.concatenate([jnp.where(live_far, mass_b, 0.0), blank], axis=1)
            moment_b = jnp.concatenate([jnp.where(live_far, moment_b, 0.0), blank], axis=1)
        highest = jnp.maximum(top, top_b)
        share_a = jnp.exp(top - highest)
        share_b = jnp.exp(top_b - highest)
        norm = 1.0 / (mass * share_a + mass_b * share_b)
        delta = (moment * share_a + moment_b * share_b) * norm
        factor = share_a * norm
        if not kind:
            factor = jnp.where(live_far, factor, 0.0)
        probs = expd * factor
        dscores = probs * (dprobs - delta)
        return split(probs, 2), split(dscores, 2)

    def key_terms(image, first, size, probs, dscores):
        lanes = slice(first, first + size)
        stacked = [qs[image, index, lanes] for index in range(2)]
        dkeys = product(dscores, stacked, THREE, ((1,), (0,)))
        stacked = [cs[image, index, lanes] for index in range(2)]
        return dkeys, product(probs, stacked, THREE, ((1,), (0,)))

    for image in range(images):
        stack_own(image)
    parts, own_kept, far_kept, far_terms, own_grads = [], [], [], [], []
    for image in range(images):
        for side in range(2):
            pl.when(has[side])(col_copy(image, 1 - side).wait_recv)
        parts.append((split(kv[image, 0], 3), split(kv[image, 1], 2)))
        own_kept.append(first_pass(image, 0, HALF, *parts[image]))
    for image in range(images):
        row_copy(image).wait_recv()
        stack_halo(image)
        far_kept.append(first_pass(image, OWN, LANES - OWN, *parts[image]))
    for image in range(images):
        rest = first_pass(image, HALF, HALF, *parts[image])
        own_kept[image] = [jnp.concatenate(pair, axis=1) for pair in zip(own_kept[image], rest)]
    for image in range(images):
        far_kept[image] = weights(image, OWN, LANES - OWN, *far_kept[image])
        spread = product(far_kept[image][1], parts[image][0], THREE, ((0,), (0,)))
        part_out[image] = fold(spread, SLOTS)[:EDGE] * SCALE
        part_copy(image).start()
    for image in range(images):
        far_terms.append(key_terms(image, OWN, LANES - OWN, *far_kept[image]))
    for image in range(images):
        own_kept[image] = weights(image, 0, OWN, *own_kept[image])
        dkeys, dvalues = key_terms(image, 0, OWN, *own_kept[image])
        dkeys = dkeys + far_terms[image][0]
        dvalues = dvalues + far_terms[image][1]
        for side, first in enumerate((LEFT, RIGHT)):
            terms[image, side, 0] = dkeys[first : first + EDGE]
            terms[image, side, 1] = dvalues[first : first + EDGE]
            pl.when(has[side])(term_copy(image, side).start)
        own_grads.append((dkeys[:tokens], dvalues[:tokens]))
    for image in range(images):
        dk_ref[image], dv_ref[image] = own_grads[image]
        spread = product(own_kept[image][1], parts[image][0], THREE, ((0,), (0,)))
        own = [fold(spread[:HALF], SLOTS), fold(spread[HALF:], SLOTS)]
        own = jnp.concatenate(own, axis=0) * SCALE
        for row in range(TILE):
            dq_ref[image, turned(row)] = own[row * TILE : (row + 1) * TILE]

    def add(image, side):
        term_copy(image, 1 - side).wait_recv()
        for field, ref in enumerate((dk_ref, dv_ref)):
            for row in range(TILE):
                at = row * TILE + cut[side].start
                ref[image, at : at + 3] += back[image, 1 - side, field, 3 * row : 3 * row + 3]

    for image in range(images):
        part_copy(image).wait_recv()
        dq_ref[image, pl.ds(edge_start, EDGE)] += part_in[image]
    even = lax.rem(wa, 2) == 0
    for parity, order in ((even, (1, 0)), (jnp.logical_not(even), (0, 1))):
        for side in order:
            for image in range(images):
                pl.when(jnp.logical_and(has[side], parity))(functools.partial(add, image, side))

    for image in range(images):
        row_copy(image).wait_send()
        for kind in range(2):
            sheet_copy(image, kind).wait_send()
        part_copy(image).wait_send()
        for side in range(2):
            pl.when(has[side])(col_copy(image, side).wait_send)
            pl.when(has[side])(term_copy(image, side).wait_send)


def store(*refs):
    sem = refs[6]
    copies = [pltpu.make_async_copy(refs[i], refs[3 + i], sem.at[i]) for i in range(3)]
    for copy in copies:
        copy.start()
    for copy in copies:
        copy.wait()


def per_device(wa_count, queries, keys, values, cotangent):
    images, tile_rows, tile_cols, channels = queries.shape
    flat = (images, tile_rows * tile_cols, channels)
    f32, bf16 = jnp.float32, jnp.bfloat16
    out = jax.ShapeDtypeStruct(flat, f32)
    sems = pltpu.SemaphoreType.DMA
    results = pl.pallas_call(
        functools.partial(kernel, wa_count),
        out_shape=(pltpu.VMEM(flat, f32),) * 3,
        in_specs=[pl.BlockSpec(memory_space=pl.ANY)] * 4,
        out_specs=(pl.BlockSpec(memory_space=pltpu.VMEM),) * 3,
        scratch_shapes=[
            pltpu.VMEM((images, 2, WIDE, channels), f32),
            pltpu.VMEM((images, 2, TOKENS, channels), f32),
            pltpu.VMEM((images, 2, SLOTS, channels), f32),
            pltpu.VMEM((images, 2, 2, EDGE, channels), f32),
            pltpu.VMEM((WIDE, LANES), f32),
            pltpu.VMEM((images, 2, LANES, channels), bf16),
            pltpu.VMEM((images, 2, LANES, channels), bf16),
            pltpu.VMEM((images, 3, channels, LANES), bf16),
            pltpu.VMEM((images, 2, channels, LANES), bf16),
            pltpu.VMEM((images, 2, 8, 128), f32),
            pltpu.VMEM((images, 2, 8, 128), f32),
            pltpu.VMEM((images, 2, 2, EDGE, channels), f32),
            pltpu.VMEM((images, 2, 2, EDGE, channels), f32),
            pltpu.VMEM((images, EDGE, channels), f32),
            pltpu.VMEM((images, EDGE, channels), f32),
            sems((4,)),
            sems((2, images)),
            sems((2, images, 2)),
            sems((2, images, 2)),
            sems((2, images, 2)),
            sems((2, images)),
        ],
        compiler_params=pltpu.CompilerParams(collective_id=0, has_side_effects=True),
    )(*(x.reshape(flat) for x in (queries, keys, values, cotangent)))
    results = pl.pallas_call(
        store,
        out_shape=(out, out, out),
        in_specs=[pl.BlockSpec(memory_space=pltpu.VMEM)] * 3,
        out_specs=(pl.BlockSpec(memory_space=pl.ANY),) * 3,
        scratch_shapes=[sems((3,))],
    )(*(pltpu.with_memory_space_constraint(x, pltpu.VMEM) for x in results))
    return tuple(x.reshape(queries.shape) for x in results)


def solution(mesh):
    spec = P(None, "ha", "wa", None)
    return jax.shard_map(
        functools.partial(per_device, mesh.shape["wa"]),
        mesh=mesh,
        in_specs=(spec,) * 4,
        out_specs=(spec,) * 3,
        check_vma=False,
    )
```

```python
import functools

import jax
import jax.numpy as jnp
from jax import lax
from jax.experimental import pallas as pl
from jax.experimental.pallas import tpu as pltpu
from jax.sharding import PartitionSpec as P

HEADS = 4
REACH = 3
MESH = pl.DeviceIdType.MESH

TILE = 8
TOKENS = 64
EDGE = REACH * TILE
LEFT = 64
RIGHT = 88
WIDE = 112
OWN = 256
HALF = 128
SLOTS = 32
LANES = 384
SCALE = 1.0 / 8.0
FAR = -1e30


def dot(a, b, contract):
    return lax.dot_general(a, b, (contract, ((), ())), preferred_element_type=jnp.float32)


def split(x, parts):
    out = []
    for index in range(parts):
        part = x.astype(jnp.bfloat16)
        out.append(part)
        if index + 1 < parts:
            x = x - part.astype(jnp.float32)
    return out


def beside(parts, order):
    return jnp.concatenate([parts[index] for index in order], axis=1)


def below(parts, order):
    return jnp.concatenate([parts[index] for index in order], axis=0)


def product(a, b, order, contract):
    left = beside if contract[0][0] else below
    right = beside if contract[1][0] else below
    return dot(left(a, [i for i, _ in order]), right(b, [j for _, j in order]), contract)


SIX = ((2, 0), (0, 2), (1, 1), (1, 0), (0, 1), (0, 0))
THREE = ((1, 0), (0, 1), (0, 0))


def third(index):
    return (index * 11) >> 5


def kernel(
    wa_count,
    q_hbm,
    k_hbm,
    v_hbm,
    c_hbm,
    dq_ref,
    dk_ref,
    dv_ref,
    kv,
    qc,
    halo,
    packed,
    bias,
    qs,
    cs,
    qt,
    ct,
    sheet_out,
    sheet_in,
    terms,
    back,
    part_out,
    part_in,
    load_sem,
    row_sem,
    col_sem,
    sheet_sem,
    term_sem,
    part_sem,
):
    images, tokens, channels = q_hbm.shape
    head_size = channels // HEADS
    ha = lax.axis_index("ha")
    wa = lax.axis_index("wa")
    other = 1 - ha
    has = (wa > 0, wa < wa_count - 1)
    side_device = ((ha, jnp.maximum(wa - 1, 0)), (ha, jnp.minimum(wa + 1, wa_count - 1)))
    partner = (other, wa)

    barrier = pltpu.get_barrier_semaphore()

    def greet(device):
        pl.semaphore_signal(barrier, inc=1, device_id=device, device_id_type=MESH)

    greet(partner)
    for side in range(2):
        pl.when(has[side])(functools.partial(greet, side_device[side]))

    loads = {}
    for name, ref, target in (
        ("k", k_hbm, kv.at[:, 0, pl.ds(0, tokens)]),
        ("v", v_hbm, kv.at[:, 1, pl.ds(0, tokens)]),
        ("q", q_hbm, qc.at[:, 0]),
        ("c", c_hbm, qc.at[:, 1]),
    ):
        loads[name] = pltpu.make_async_copy(ref, target, load_sem.at[len(loads)])
        loads[name].start()

    edge = (TILE - REACH) * other

    def iota(shape, dim):
        return lax.broadcasted_iota(jnp.int32, shape, dim)

    lane = iota((1, LANES), 1)
    slot = lane & (SLOTS - 1)
    slot = jnp.where((lane >= HALF) & (lane < OWN), slot + SLOTS, slot)
    own_row = ((slot >> 3) + edge) & (TILE - 1)
    far_row = jnp.where(slot < EDGE, jnp.where(ha == 0, TILE, -REACH) + (slot >> 3), 100)
    query_row = jnp.where(lane < OWN, own_row, far_row)
    query_col = slot & (TILE - 1)
    for first, size in ((0, tokens), (LEFT, EDGE), (RIGHT, EDGE)):
        index = iota((size, 1), 0)
        if first == 0:
            row, col = index >> 3, index & (TILE - 1)
        else:
            row = third(index)
            col = index - 3 * row + (-REACH if first == LEFT else TILE)
            row = row + jnp.where(has[0 if first == LEFT else 1], 0, 1000)
        gap = jnp.maximum(jnp.abs(row - query_row), jnp.abs(col - query_col))
        bias[first : first + size] = jnp.where(gap <= REACH, 0.0, FAR)
    for image in range(images):
        for field in range(2):
            halo[image, field, EDGE:SLOTS] = jnp.zeros((SLOTS - EDGE, channels), jnp.float32)

    def clear(first):
        for image in range(images):
            for field in range(2):
                kv[image, field, first : first + EDGE] = jnp.zeros((EDGE, channels), jnp.float32)

    pl.when(jnp.logical_not(has[0]))(lambda: clear(LEFT))
    pl.when(jnp.logical_not(has[1]))(lambda: clear(RIGHT))

    cut = (slice(0, REACH), slice(TILE - REACH, TILE))

    def pack():
        for name in "kvqc":
            loads[name].wait()
        for image in range(images):
            for field in range(2):
                mine = kv[image, field, 0:tokens]
                for row in range(TILE):
                    line = mine[row * TILE : (row + 1) * TILE]
                    for side in range(2):
                        packed[image, side, field, 3 * row : 3 * row + 3] = line[cut[side]]

    pack()
    pl.semaphore_wait(barrier, 1 + has[0].astype(jnp.int32) + has[1].astype(jnp.int32))

    def remote(source, target, sems, index, device):
        return pltpu.make_async_remote_copy(
            src_ref=source,
            dst_ref=target,
            send_sem=sems.at[(0,) + index],
            recv_sem=sems.at[(1,) + index],
            device_id=device,
            device_id_type=MESH,
        )

    edge_start = pl.multiple_of(edge * TILE, TILE)

    def row_copy(image):
        source = qc.at[image, :, pl.ds(edge_start, EDGE)]
        return remote(source, halo.at[image, :, pl.ds(0, EDGE)], row_sem, (image,), partner)

    def col_copy(image, side):
        target = kv.at[image, :, pl.ds((RIGHT, LEFT)[side], EDGE)]
        return remote(packed.at[image, side], target, col_sem, (image, side), side_device[side])

    def sheet_copy(image, kind):
        source, target = sheet_out.at[image, kind], sheet_in.at[image, kind]
        return remote(source, target, sheet_sem, (image, kind), partner)

    def term_copy(image, side):
        source, target = terms.at[image, side], back.at[image, side]
        return remote(source, target, term_sem, (image, side), side_device[side])

    def part_copy(image):
        return remote(part_out.at[image], part_in.at[image], part_sem, (image,), partner)

    for image in range(images):
        row_copy(image).start()
        for side in range(2):
            pl.when(has[side])(col_copy(image, side).start)

    lane_head = iota((tokens, channels), 1) // head_size
    heads = [jnp.where(lane_head == head, 1.0, 0.0).astype(jnp.bfloat16) for head in range(HEADS)]

    def turned(row):
        return pl.ds(pl.multiple_of(((row + edge) & (TILE - 1)) * TILE, TILE), TILE)

    def stack(image, first, blocks):
        for x, rows, columns, count in ((blocks[0] * SCALE, qs, qt, 3), (blocks[1], cs, ct, 2)):
            size = x.shape[0]
            lanes = slice(first, first + HEADS * size)
            for index, part in enumerate(split(x, 2)):
                for head in range(HEADS):
                    base = first + head * size
                    rows[image, index, base : base + size] = part * heads[head][:size]
            spread = [jnp.where(lane_head[:size] == head, x, 0.0) for head in range(HEADS)]
            turned_x = jnp.transpose(jnp.concatenate(spread, axis=0))
            for index, part in enumerate(split(turned_x, count)):
                columns[image, index, :, lanes] = part

    def stack_own(image):
        for half in range(2):
            lines = range(half * SLOTS // TILE, (half + 1) * SLOTS // TILE)
            blocks = [
                jnp.concatenate([qc[image, field, turned(row)] for row in lines], axis=0)
                for field in range(2)
            ]
            stack(image, half * HALF, blocks)

    def stack_halo(image):
        stack(image, OWN, [halo[image, field] for field in range(2)])

    def first_pass(image, first, size, keys, values):
        lanes = slice(first, first + size)
        stacked = [qt[image, index, :, lanes] for index in range(3)]
        scores = product(keys, stacked, SIX, ((1,), (0,))) + bias[:, lanes]
        stacked = [ct[image, index, :, lanes] for index in range(2)]
        dprobs = product(values, stacked, THREE, ((1,), (0,)))
        top = jnp.max(scores, axis=0, keepdims=True)
        expd = jnp.exp(scores - top)
        mass = jnp.sum(expd, axis=0, keepdims=True)
        moment = jnp.sum(expd * dprobs, axis=0, keepdims=True)
        sheet = jnp.concatenate([top, mass, moment, jnp.zeros((5, size), jnp.float32)], axis=0)
        if first != HALF:
            kind = int(first == OWN)
            sheet_out[image, kind] = sheet
            sheet_copy(image, kind).start()
        return expd, dprobs, top, mass, moment

    def fold(stacked, size):
        total = jnp.zeros((size, channels), jnp.float32)
        for head in range(HEADS):
            total = total + jnp.where(
                lane_head[:size] == head, stacked[head * size : (head + 1) * size], 0.0
            )
        return total

    live_far = (iota((1, 128), 1) & (SLOTS - 1)) < EDGE

    def weights(image, first, size, expd, dprobs, top, mass, moment):
        kind = int(first != OWN)
        sheet_copy(image, kind).wait_recv()
        sheet = sheet_in[image, kind]
        top_b, mass_b, moment_b = sheet[0:1], sheet[1:2], sheet[2:3]
        if kind:
            blank = jnp.zeros((1, HALF), jnp.float32)
            top_b = jnp.concatenate([jnp.where(live_far, top_b, FAR), blank + FAR], axis=1)
            mass_b = jnp.concatenate([jnp.where(live_far, mass_b, 0.0), blank], axis=1)
            moment_b = jnp.concatenate([jnp.where(live_far, moment_b, 0.0), blank], axis=1)
        highest = jnp.maximum(top, top_b)
        share_a = jnp.exp(top - highest)
        share_b = jnp.exp(top_b - highest)
        norm = 1.0 / (mass * share_a + mass_b * share_b)
        delta = (moment * share_a + moment_b * share_b) * norm
        factor = share_a * norm
        if not kind:
            factor = jnp.where(live_far, factor, 0.0)
        probs = expd * factor
        dscores = probs * (dprobs - delta)
        return split(probs, 2), split(dscores, 2)

    def key_terms(image, first, size, probs, dscores):
        lanes = slice(first, first + size)
        stacked = [qs[image, index, lanes] for index in range(2)]
        dkeys = product(dscores, stacked, THREE, ((1,), (0,)))
        stacked = [cs[image, index, lanes] for index in range(2)]
        return dkeys, product(probs, stacked, THREE, ((1,), (0,)))

    for image in range(images):
        stack_own(image)
    parts, own_kept, far_kept, far_terms, own_grads = [], [], [], [], []
    for image in range(images):
        for side in range(2):
            pl.when(has[side])(col_copy(image, 1 - side).wait_recv)
        parts.append((split(kv[image, 0], 3), split(kv[image, 1], 2)))
        own_kept.append(first_pass(image, 0, HALF, *parts[image]))
    for image in range(images):
        row_copy(image).wait_recv()
        stack_halo(image)
        far_kept.append(first_pass(image, OWN, LANES - OWN, *parts[image]))
    for image in range(images):
        far_kept[image] = weights(image, OWN, LANES - OWN, *far_kept[image])
        spread = product(far_kept[image][1], parts[image][0], THREE, ((0,), (0,)))
        part_out[image] = fold(spread, SLOTS)[:EDGE] * SCALE
        part_copy(image).start()
    for image in range(images):
        rest = first_pass(image, HALF, HALF, *parts[image])
        own_kept[image] = [jnp.concatenate(pair, axis=1) for pair in zip(own_kept[image], rest)]
    for image in range(images):
        far_terms.append(key_terms(image, OWN, LANES - OWN, *far_kept[image]))
    for image in range(images):
        own_kept[image] = weights(image, 0, OWN, *own_kept[image])
        dkeys, dvalues = key_terms(image, 0, OWN, *own_kept[image])
        dkeys = dkeys + far_terms[image][0]
        dvalues = dvalues + far_terms[image][1]
        for side, first in enumerate((LEFT, RIGHT)):
            terms[image, side, 0] = dkeys[first : first + EDGE]
            terms[image, side, 1] = dvalues[first : first + EDGE]
            pl.when(has[side])(term_copy(image, side).start)
        own_grads.append((dkeys[:tokens], dvalues[:tokens]))
    for image in range(images):
        dk_ref[image], dv_ref[image] = own_grads[image]
        spread = product(own_kept[image][1], parts[image][0], THREE, ((0,), (0,)))
        own = [fold(spread[:HALF], SLOTS), fold(spread[HALF:], SLOTS)]
        own = jnp.concatenate(own, axis=0) * SCALE
        for row in range(TILE):
            dq_ref[image, turned(row)] = own[row * TILE : (row + 1) * TILE]

    def add(image, side):
        term_copy(image, 1 - side).wait_recv()
        for field, ref in enumerate((dk_ref, dv_ref)):
            for row in range(TILE):
                at = row * TILE + cut[side].start
                ref[image, at : at + 3] += back[image, 1 - side, field, 3 * row : 3 * row + 3]

    for image in range(images):
        part_copy(image).wait_recv()
        dq_ref[image, pl.ds(edge_start, EDGE)] += part_in[image]
    even = lax.rem(wa, 2) == 0
    for parity, order in ((even, (1, 0)), (jnp.logical_not(even), (0, 1))):
        for side in order:
            for image in range(images):
                pl.when(jnp.logical_and(has[side], parity))(functools.partial(add, image, side))

    for image in range(images):
        row_copy(image).wait_send()
        for kind in range(2):
            sheet_copy(image, kind).wait_send()
        part_copy(image).wait_send()
        for side in range(2):
            pl.when(has[side])(col_copy(image, side).wait_send)
            pl.when(has[side])(term_copy(image, side).wait_send)


def store(*refs):
    sem = refs[6]
    copies = [pltpu.make_async_copy(refs[i], refs[3 + i], sem.at[i]) for i in range(3)]
    for copy in copies:
        copy.start()
    for copy in copies:
        copy.wait()


def per_device(wa_count, queries, keys, values, cotangent):
    images, tile_rows, tile_cols, channels = queries.shape
    flat = (images, tile_rows * tile_cols, channels)
    f32, bf16 = jnp.float32, jnp.bfloat16
    out = jax.ShapeDtypeStruct(flat, f32)
    sems = pltpu.SemaphoreType.DMA
    results = pl.pallas_call(
        functools.partial(kernel, wa_count),
        out_shape=(pltpu.VMEM(flat, f32),) * 3,
        in_specs=[pl.BlockSpec(memory_space=pl.ANY)] * 4,
        out_specs=(pl.BlockSpec(memory_space=pltpu.VMEM),) * 3,
        scratch_shapes=[
            pltpu.VMEM((images, 2, WIDE, channels), f32),
            pltpu.VMEM((images, 2, TOKENS, channels), f32),
            pltpu.VMEM((images, 2, SLOTS, channels), f32),
            pltpu.VMEM((images, 2, 2, EDGE, channels), f32),
            pltpu.VMEM((WIDE, LANES), f32),
            pltpu.VMEM((images, 2, LANES, channels), bf16),
            pltpu.VMEM((images, 2, LANES, channels), bf16),
            pltpu.VMEM((images, 3, channels, LANES), bf16),
            pltpu.VMEM((images, 2, channels, LANES), bf16),
            pltpu.VMEM((images, 2, 8, 128), f32),
            pltpu.VMEM((images, 2, 8, 128), f32),
            pltpu.VMEM((images, 2, 2, EDGE, channels), f32),
            pltpu.VMEM((images, 2, 2, EDGE, channels), f32),
            pltpu.VMEM((images, EDGE, channels), f32),
            pltpu.VMEM((images, EDGE, channels), f32),
            sems((4,)),
            sems((2, images)),
            sems((2, images, 2)),
            sems((2, images, 2)),
            sems((2, images, 2)),
            sems((2, images)),
        ],
        compiler_params=pltpu.CompilerParams(collective_id=0, has_side_effects=True),
    )(*(x.reshape(flat) for x in (queries, keys, values, cotangent)))
    results = pl.pallas_call(
        store,
        out_shape=(out, out, out),
        in_specs=[pl.BlockSpec(memory_space=pltpu.VMEM)] * 3,
        out_specs=(pl.BlockSpec(memory_space=pl.ANY),) * 3,
        scratch_shapes=[sems((3,))],
    )(*(pltpu.with_memory_space_constraint(x, pltpu.VMEM) for x in results))
    return tuple(x.reshape(queries.shape) for x in results)


def solution(mesh):
    spec = P(None, "ha", "wa", None)
    return jax.shard_map(
        functools.partial(per_device, mesh.shape["wa"]),
        mesh=mesh,
        in_specs=(spec,) * 4,
        out_specs=(spec,) * 3,
        check_vma=False,
    )
```
